128 devices in a mesh: dom: 8 (over y_hi, z), blk: 16 (over y_lo, x, core).
Axes of the slice: x: 4, y: 4 (y_hi: 2, y_lo: 2; y = y_hi * 2 + y_lo), z: 4, core: 2. Of those that a mesh axis runs over, the one named last changes fastest.
Arguments:
- features_domain: bfloat16 [98304, 1152], P(('dom', 'blk')), may hold values from -6 to 6
- arrival: int32 [98304], P(('dom', 'blk')), may hold values from 0 to 767, as said below
- positions: float32 [98304, 3], P(('dom', 'blk')), may hold values from 0 to 3072, as said below
- species: int32 [98304], P(('dom', 'blk')), may hold values from 0 to 88
- block_count: int32 [1536], P(('dom', 'blk')), may hold values from 16 to 64, as said below
- pair_block: int32 [1536, 3], P(('dom', 'blk')), may hold values from -1 to 1535, as said below
- radial_weights: float32 [8, 7, 128], replicated, may hold values from -0.75 to 0.75
- species_weights: float32 [89, 3, 128], replicated, may hold values from -1 to 1
- mix_weight: bfloat16 [128, 128], replicated, may hold values from -0.5 to 0.5
- self_weight: bfloat16 [128, 128], replicated, may hold values from -0.5 to 0.5
- readout: float32 [128], replicated, may hold values from -0.5 to 0.5
Outputs:
- atom_energy: float32 [98304], P(('dom', 'blk'))
- forces: float32 [98304, 3], P(('dom', 'blk'))
- new_features: bfloat16 [98304, 128], P(('dom', 'blk'))
The draws below stay inside these ranges and needn't reach their ends.
Inputs may be any that keep to these rules, and one draw needn't show every extreme that they name: `arrival`: on each device of dom+blk its 768 entries are a permutation of 0 to 767. `pair_block`: entry [b, 0] is b - 1 or -1, entry [b, 1] is b, entry [b, 2] is b + 1 or -1; the lists are symmetric: [b, 2] is b + 1 exactly when [b + 1, 0] is b. The first block has no predecessor and the last no successor. `block_count`: the live atoms of a block are its first slots. `positions`: atoms of blocks that are not paired lie a distance of 1 or more apart.
All inputs are finite; a program needn't handle non-finite values.
Results may differ from the reference program's by a relative error of at most 0.015.
Values may be sent and summed in bfloat16 or wider, within the bound.
A program may use at most 64 MiB of HBM per device.

```python
import math
import jax
import jax.numpy as jnp
import numpy as np
from jax import lax

C = 128
NB = 8
SPEC = 89
HARM = 9
BLOCK = 64
ATOM_DEV = 768
NDEV = 128
PIECE = 6
ATOMS = 98304
NBLOCKS = 1536


def gap_marks_of(key):
    draw_flags = jax.random.randint(jax.random.fold_in(key, 11), (NBLOCKS,), 0, 4)
    gap_marks = (draw_flags == 0).astype(jnp.int32)
    return gap_marks.at[NBLOCKS - 1].set(1)


def draw_pair_block(key, part):
    gap_marks = gap_marks_of(key)
    blocks = jnp.arange(NBLOCKS, dtype=jnp.int32)
    before = jnp.concatenate([jnp.ones((1,), jnp.int32), gap_marks[:-1]])
    left_pair = jnp.where(before == 0, blocks - 1, -1)
    right_pair = jnp.where(gap_marks == 0, blocks + 1, -1)
    return jnp.stack([left_pair, blocks, right_pair], axis=1).astype(jnp.int32)


def draw_positions(key, part):
    gap_marks = gap_marks_of(key)
    blocks = jnp.arange(NBLOCKS, dtype=jnp.int32)
    anchor = (blocks + jnp.cumsum(gap_marks) - gap_marks).astype(jnp.float32)
    offsets = jax.random.uniform(jax.random.fold_in(key, 12), (NBLOCKS, BLOCK, 3), jnp.float32)
    along_axis = anchor[:, None] + offsets[:, :, 0]
    across = 1.5 * offsets[:, :, 1]
    upward = 1.5 * offsets[:, :, 2]
    return jnp.stack([along_axis, across, upward], axis=2).reshape(NBLOCKS * BLOCK, 3).astype(jnp.float32)


def draw_block_count(key, part):
    counts = jax.random.randint(jax.random.fold_in(key, 13), (NBLOCKS,), 16, BLOCK)
    per_device = NBLOCKS // NDEV
    chosen = jax.random.randint(jax.random.fold_in(key, 14), (NDEV, 1), 0, per_device)
    count_grid = counts.reshape(NDEV, per_device)
    filled = jnp.where(jnp.arange(per_device)[None, :] == chosen, BLOCK, count_grid)
    return filled.reshape(NBLOCKS).astype(jnp.int32)


def draw_arrival(key, part):
    device_keys = jax.random.split(jax.random.fold_in(key, 15), NDEV)

    def shuffled(single):
        return jax.random.permutation(single, ATOM_DEV)
    orders = jax.vmap(shuffled)(device_keys)
    return orders.reshape(NDEV * ATOM_DEV).astype(jnp.int32)


def touch_ends(drawn, own_key, low, top_value):
    place = [jax.random.randint(jax.random.fold_in(own_key, axis), (), 0, length) for axis, length in enumerate(drawn.shape)]
    widest = drawn.shape.index(max(drawn.shape))
    neighbour = place[:widest] + [(place[widest] + 1) % drawn.shape[widest]] + place[widest + 1:]
    return drawn.at[tuple(place)].set(low).at[tuple(neighbour)].set(top_value)


def shard_levels(rng, dims, shards, low, largest):
    gain = 1.0
    for position, blocks in shards:
        steps = jax.random.uniform(jax.random.fold_in(jax.random.fold_in(rng, 6), position), (blocks,), jnp.float32, low / len(shards), largest / len(shards))
        gain = gain * jnp.repeat(jnp.exp(steps), dims[position] // blocks).reshape((-1,) + (1,) * (len(dims) - 1 - position))
    return gain


def scatter_about(own_key, extent, deviation, most, cuts=(), kind=jnp.bfloat16):
    values = jax.random.normal(own_key, extent, jnp.float32) * deviation
    if len(cuts) > 0:
        values = shard_levels(own_key, extent, cuts, -0.22, 0.18) * values
    return jnp.clip(values, min=-most, max=most).astype(kind)


def setup_inputs(seed: int = 0) -> dict:
    splits = jax.random.split(jax.random.key(seed), 12)
    features_domain = scatter_about(splits[0], (ATOMS, HARM * C), 1.0, 6.0, ((0, 128),))
    arrival = draw_arrival(jax.random.fold_in(splits[11], 71), 0)
    positions = draw_positions(jax.random.fold_in(splits[11], 71), 0)
    species = touch_ends(jax.random.randint(splits[3], (ATOMS,), 0, SPEC), jax.random.fold_in(splits[3], 1), 0, SPEC - 1).astype(jnp.int32)
    block_count = draw_block_count(jax.random.fold_in(splits[11], 71), 0)
    pair_block = draw_pair_block(jax.random.fold_in(splits[11], 71), 0)
    radial_weights = scatter_about(splits[6], (NB, 7, C), 64 ** -0.5, 0.75, (), jnp.float32)
    species_weights = jnp.clip(jax.random.uniform(splits[7], (SPEC, 3, C), jnp.float32, -1.0, 1.0), -1.0, 1.0)
    mix_weight = scatter_about(splits[8], (C, C), C ** -0.5, 0.5)
    self_weight = scatter_about(splits[9], (C, C), C ** -0.5, 0.5)
    readout = scatter_about(splits[10], (C,), C ** -0.5, 0.5, (), jnp.float32)
    return {"features_domain": features_domain, "arrival": arrival, "positions": positions, "species": species, "block_count": block_count, "pair_block": pair_block, "radial_weights": radial_weights, "species_weights": species_weights, "mix_weight": mix_weight, "self_weight": self_weight, "readout": readout}


ROOT_THREE = math.sqrt(3.0)
DOT_PATH = np.array([0, 5, 5, 5, 6, 6, 6, 6, 6])
CARRY_PATH = np.array([3, 3, 3, 4, 4, 4, 4, 4])

def harmonics(delta_x, delta_y, delta_z):
    return jnp.stack([jnp.ones_like(delta_x), delta_x, delta_y, delta_z, ROOT_THREE * delta_x * delta_y, ROOT_THREE * delta_y * delta_z, 0.5 * (2.0 * delta_z * delta_z - delta_x * delta_x - delta_y * delta_y), ROOT_THREE * delta_z * delta_x, 0.5 * ROOT_THREE * (delta_x * delta_x - delta_y * delta_y)])

def pair_mask(pair_row, block_rows):
    columns = jnp.arange(3 * block_rows, dtype=jnp.int32)
    listed = (pair_row >= 0).astype(jnp.float32)
    slot_mask = jnp.where(columns < block_rows, listed[0], jnp.where(columns < 2 * block_rows, listed[1], listed[2]))
    targets = jnp.arange(block_rows, dtype=jnp.int32)[:, None] + block_rows
    distinct = (targets != columns[None, :]).astype(jnp.float32)
    return slot_mask[None, :] * distinct

def edge_factors(window_pos, pair_keep, basis_count):
    block_rows = pair_keep.shape[0]
    coords = window_pos.T
    centre = coords[:, block_rows:2 * block_rows]
    delta_x = coords[0][None, :] - centre[0][:, None]
    delta_y = coords[1][None, :] - centre[1][:, None]
    delta_z = coords[2][None, :] - centre[2][:, None]
    spread = delta_x * delta_x + delta_y * delta_y + delta_z * delta_z
    envelope = jnp.maximum(1.0 - spread, 0.0) ** 3 * pair_keep
    orders = jnp.arange(basis_count, dtype=jnp.float32) * math.pi
    radial = envelope[None] * jnp.cos(orders[:, None, None] * spread[None])
    return (radial[:, None] * harmonics(delta_x, delta_y, delta_z)[None]).astype(jnp.bfloat16)

def feature_terms(window_feat, radial_weights):
    values = window_feat.astype(jnp.float32)
    dot_terms = (radial_weights[:, None, DOT_PATH, :] * values[None]).astype(jnp.bfloat16)
    lift_terms = (radial_weights[:, None, 1:3, :] * values[None, :, 0:1, :]).astype(jnp.bfloat16)
    carry_terms = (radial_weights[:, None, CARRY_PATH, :] * values[None, :, 1:, :]).astype(jnp.bfloat16)
    return (dot_terms, lift_terms, carry_terms)

def widen(terms):
    return lax.optimization_barrier(terms).astype(jnp.float32)

def block_messages(edges, dot_terms, lift_terms, carry_terms):
    exact = lax.Precision.HIGHEST
    wide_edges = edges.astype(jnp.float32)
    wide_lift = widen(lift_terms)
    scalar = jnp.einsum('nyij,njyc->ic', wide_edges, widen(dot_terms), precision=exact)
    first_order = jnp.einsum('nmij,njc->mic', wide_edges[:, 1:4], wide_lift[:, :, 0], precision=exact)
    second = jnp.einsum('nmij,njc->mic', wide_edges[:, 4:9], wide_lift[:, :, 1], precision=exact)
    carried = jnp.einsum('nij,njyc->yic', wide_edges[:, 0], widen(carry_terms), precision=exact)
    return jnp.concatenate([scalar[None], first_order + carried[0:3], second + carried[3:8]], axis=0)

def atom_outputs(message_rows, gain_rows, self_part, live_rows, mix_weight, self_weight, readout):
    squares = message_rows * message_rows
    basis_rows = message_rows[0] + gain_rows[:, 0] * squares[0] + gain_rows[:, 1] * lax.optimization_barrier(jnp.sum(squares[1:4], axis=0)) + gain_rows[:, 2] * lax.optimization_barrier(jnp.sum(squares[4:9], axis=0))
    rounded = basis_rows.astype(jnp.bfloat16)
    mixed_rows = jnp.dot(rounded, mix_weight, preferred_element_type=jnp.float32) + jnp.dot(self_part, self_weight, preferred_element_type=jnp.float32)
    energy = live_rows * lax.optimization_barrier(jnp.sum(readout[None, :] * jax.nn.silu(mixed_rows), axis=1))
    return (energy, (mixed_rows * live_rows[:, None]).astype(jnp.bfloat16))

def block_outputs(window_pos, window_feat, pair_row, gain_rows, live_rows, radial_weights, mix_weight, self_weight, readout):
    block_rows = gain_rows.shape[0]
    pair_keep = pair_mask(pair_row, block_rows)
    dot_terms, lift_terms, carry_terms = feature_terms(window_feat, radial_weights)

    def messages_of(positions_window):
        edges = edge_factors(positions_window, pair_keep, radial_weights.shape[0])
        return block_messages(edges, dot_terms, lift_terms, carry_terms)
    messages, pull_edges = jax.vjp(messages_of, window_pos)
    self_rows = window_feat[block_rows:2 * block_rows, 0, :]

    def outputs_of(message_rows):
        return atom_outputs(message_rows, gain_rows, self_rows, live_rows, mix_weight, self_weight, readout)
    energy, pull_atoms, features_out = jax.vjp(outputs_of, messages, has_aux=True)
    grad_messages, = pull_atoms(jnp.ones_like(energy))
    grad_window, = pull_edges(grad_messages)
    return (energy, features_out, grad_window)

def reference(features_domain, arrival, positions, species, block_count, pair_block, radial_weights, species_weights, mix_weight, self_weight, readout):
    slot_index = jnp.arange(ATOMS, dtype=jnp.int32)
    device = slot_index // ATOM_DEV
    source_row = arrival // PIECE * ATOM_DEV + device * PIECE + arrival % PIECE
    live_slots = (slot_index % BLOCK < jnp.repeat(block_count, BLOCK)).astype(jnp.int32)
    relaid = jnp.where(live_slots[:, None] > 0, features_domain[source_row], jnp.zeros((), features_domain.dtype))
    feature_view = jnp.pad(relaid, ((BLOCK, BLOCK), (0, 0))).reshape(ATOMS + 2 * BLOCK, 9, -1)
    position_ext = jnp.pad(positions, ((BLOCK, BLOCK), (0, 0)))
    live_float = live_slots.astype(jnp.float32)

    def scan_step(force_ext, block_index):
        start_row = block_index * BLOCK
        window_pos = lax.dynamic_slice_in_dim(position_ext, start_row, 3 * BLOCK, 0)
        window_feat = lax.dynamic_slice_in_dim(feature_view, start_row, 3 * BLOCK, 0)
        pair_row = lax.dynamic_index_in_dim(pair_block, block_index, 0, keepdims=False)
        species_rows = lax.dynamic_slice_in_dim(species, start_row, BLOCK, 0)
        gain_rows = species_weights[species_rows]
        live_rows = lax.dynamic_slice_in_dim(live_float, start_row, BLOCK, 0)
        energy, features_out, grad_window = block_outputs(window_pos, window_feat, pair_row, gain_rows, live_rows, radial_weights, mix_weight, self_weight, readout)
        current = lax.dynamic_slice_in_dim(force_ext, start_row, 3 * BLOCK, 0)
        force_ext = lax.dynamic_update_slice_in_dim(force_ext, current + grad_window, start_row, 0)
        return (force_ext, (energy, features_out))
    force_ext, (energies, new_rows) = lax.scan(scan_step, jnp.zeros((ATOMS + 2 * BLOCK, 3), jnp.float32), jnp.arange(NBLOCKS, dtype=jnp.int32))
    forces = -force_ext[BLOCK:ATOMS + BLOCK]
    return (energies.reshape(ATOMS), forces, new_rows.reshape(ATOMS, -1))
```

```python
import functools
import math

import jax
import jax.numpy as jnp
import numpy as np
from jax import lax
from jax.experimental import pallas as pl
from jax.experimental.pallas import tpu as pltpu
from jax.sharding import PartitionSpec as P

BLOCK = 64
CH = 128
ROOT_THREE = math.sqrt(3.0)
DOT_PATH = (0, 5, 5, 5, 6, 6, 6, 6, 6)
CARRY_PATH = (-1, 3, 3, 3, 4, 4, 4, 4, 4)
LIFT_PATH = (-1, 1, 1, 1, 2, 2, 2, 2, 2)
CHUNK = 16
NB = 8
F32 = jnp.float32
BF16 = jnp.bfloat16


def mm(a, b):
    return jnp.dot(a, b, preferred_element_type=F32)


def mm_t(a, b):
    return lax.dot_general(a, b, (((1,), (1,)), ((), ())), preferred_element_type=F32)


def sin_pi(u):
    u2 = u * u
    acc = jnp.full_like(u, -(math.pi**11) / math.factorial(11))
    for power in (9, 7, 5, 3, 1):
        sign = 1.0 if power % 4 == 1 else -1.0
        acc = acc * u2 + sign * math.pi**power / math.factorial(power)
    return acc * u


def cos_pi(u):
    u2 = u * u
    acc = jnp.full_like(u, math.pi**12 / math.factorial(12))
    for power in (10, 8, 6, 4, 2, 0):
        sign = 1.0 if power % 4 == 0 else -1.0
        acc = acc * u2 + sign * math.pi**power / math.factorial(power)
    return acc


def harmonics(dx, dy, dz, x2, y2, z2):
    return (
        None,
        dx,
        dy,
        dz,
        ROOT_THREE * (dx * dy),
        ROOT_THREE * (dy * dz),
        z2 - 0.5 * (x2 + y2),
        ROOT_THREE * (dz * dx),
        (0.5 * ROOT_THREE) * (x2 - y2),
    )


def geometry(e, row0, pos_i, pos_j, keep):
    start = pl.multiple_of(e * BLOCK + row0, CHUNK)
    centre = pos_i[pl.ds(start, CHUNK), :]
    nbr = pos_j[e]
    dx = nbr[0:1, :] - centre[:, 0:1]
    dy = nbr[1:2, :] - centre[:, 1:2]
    dz = nbr[2:3, :] - centre[:, 2:3]
    x2, y2, z2 = dx * dx, dy * dy, dz * dz
    s = x2 + y2 + z2
    t = jnp.maximum(1.0 - s, 0.0)
    mask = keep[e * 3 + row0 // BLOCK]
    t2 = t * t * mask
    if row0 // BLOCK == 1:
        row = lax.broadcasted_iota(jnp.int32, (CHUNK, CH), 0) + row0 % BLOCK
        col = lax.broadcasted_iota(jnp.int32, (CHUNK, CH), 1) % BLOCK
        t2 = jnp.where(row == col, 0.0, t2)
    return dx, dy, dz, x2, y2, z2, s, t, t2


def build_edges(e, pos_i, pos_j, keep, edges):
    odd = lax.broadcasted_iota(jnp.int32, (CHUNK, CH), 1) >= BLOCK
    for row0 in range(0, 3 * BLOCK, CHUNK):
        dx, dy, dz, x2, y2, z2, s, t, t2 = geometry(e, row0, pos_i, pos_j, keep)
        env = t2 * t
        ys = harmonics(dx, dy, dz, x2, y2, z2)
        c1 = -sin_pi(jnp.minimum(s, 1.0) - 0.5)
        c2 = 2.0 * c1 * c1 - 1.0
        two_c2 = 2.0 * c2
        before = env * jnp.where(odd, c1, c2)
        now = env * jnp.where(odd, c1, 1.0)
        for m in range(4):
            cols = slice(m * CH, (m + 1) * CH)
            rows = slice(row0, row0 + CHUNK)
            edges[0, rows, cols] = now.astype(BF16)
            for k in range(1, 9):
                edges[k, rows, cols] = (now * ys[k]).astype(BF16)
            before, now = now, two_c2 * now - before


def build_terms(e, feats, weights, terms, terms0):
    for row0 in range(0, BLOCK, CHUNK):
        start = pl.multiple_of(e * BLOCK + row0, CHUNK)
        h0 = feats[pl.ds(start, CHUNK), 0:CH].astype(F32)
        for n in range(NB):
            rows = slice(n * BLOCK + row0, n * BLOCK + row0 + CHUNK)
            terms0[rows, 0:CH] = (h0 * weights[n, 0:1, :]).astype(BF16)
            for q in range(2):
                terms[rows, (8 + q) * CH : (9 + q) * CH] = (
                    h0 * weights[n, 1 + q : 2 + q, :]
                ).astype(BF16)
        for k in range(1, 9):
            hk = feats[pl.ds(start, CHUNK), k * CH : (k + 1) * CH].astype(F32)
            for n in range(NB):
                rows = slice(n * BLOCK + row0, n * BLOCK + row0 + CHUNK)
                dot_w = weights[n, DOT_PATH[k] : DOT_PATH[k] + 1, :]
                carry_w = weights[n, CARRY_PATH[k] : CARRY_PATH[k] + 1, :]
                terms[rows, (k - 1) * CH : k * CH] = (hk * dot_w).astype(BF16)
                terms0[rows, k * CH : (k + 1) * CH] = (hk * carry_w).astype(BF16)


def pair_terms(terms, k):
    q = LIFT_PATH[k] - 1
    return jnp.concatenate(
        [terms[:, (k - 1) * CH : k * CH], terms[:, (8 + q) * CH : (9 + q) * CH]], axis=1
    )


def block_kernel(
    keep,
    count,
    pos_i,
    pos_j,
    feats,
    gains,
    weights,
    mix,
    self_w,
    readout,
    cols_out,
    nbr_out,
    new_out,
    edges,
    terms,
    terms0,
    msg,
    dmsg,
    rad,
    drad,
    harm,
    gharm,
    accum,
    cols,
):
    ext_blocks = pos_j.shape[0]
    own_blocks = ext_blocks - 2
    width = 3 * BLOCK

    msg[...] = jnp.zeros_like(msg)
    dmsg[...] = jnp.zeros_like(dmsg)
    cols[...] = jnp.zeros_like(cols)

    def forward(e, carry):
        build_edges(e, pos_i, pos_j, keep, edges)
        build_terms(e, feats, weights, terms, terms0)
        rows = pl.ds(pl.multiple_of(e * BLOCK, BLOCK), width)
        total = mm(edges[0], terms0[:, 0:CH])
        for k in range(1, 9, 2):
            carried = mm(edges[0], terms0[:, k * CH : (k + 2) * CH])
            for step in range(2):
                both = mm(edges[k + step], pair_terms(terms, k + step))
                total += both[:, 0:CH]
                msg[k + step, rows, :] += both[:, CH:] + carried[:, step * CH : (step + 1) * CH]
        msg[0, rows, :] += total
        return carry

    lax.fori_loop(0, ext_blocks, forward, 0)

    def atoms(b, carry):
        rows = pl.ds(pl.multiple_of((b + 2) * BLOCK, BLOCK), BLOCK)
        own = pl.ds(pl.multiple_of(b * BLOCK, BLOCK), BLOCK)
        ext = pl.ds(pl.multiple_of((b + 1) * BLOCK, BLOCK), BLOCK)
        live = (lax.broadcasted_iota(jnp.int32, (BLOCK, 1), 0) < count[b]).astype(F32)
        m = [msg[k, rows, :] for k in range(9)]
        first = m[1] * m[1] + m[2] * m[2] + m[3] * m[3]
        second = m[4] * m[4] + m[5] * m[5] + m[6] * m[6] + m[7] * m[7] + m[8] * m[8]
        g0, g1, g2 = (gains[own, l * CH : (l + 1) * CH] for l in range(3))
        basis = m[0] + g0 * (m[0] * m[0]) + g1 * first + g2 * second
        mixed = mm(basis.astype(BF16), mix[...]) + mm(feats[ext, 0:CH], self_w[...])
        new_out[own, :] = (mixed * live).astype(BF16)
        gate = 1.0 / (1.0 + jnp.exp(-mixed))
        value = mixed * gate
        energy = live * jnp.sum(readout[...] * value, axis=1, keepdims=True)
        slope = live * readout[...] * (gate + value * (1.0 - gate))
        dbasis = mm_t(slope.astype(BF16), mix[...]).astype(BF16).astype(F32)
        dmsg[rows, 0:CH] = (dbasis * (1.0 + 2.0 * g0 * m[0])).astype(BF16)
        for k in range(1, 9):
            gain = g1 if k < 4 else g2
            dmsg[rows, k * CH : (k + 1) * CH] = (2.0 * dbasis * gain * m[k]).astype(BF16)
        lane = lax.broadcasted_iota(jnp.int32, (BLOCK, CH), 1)
        cols[rows, :] = jnp.where(lane == 3, energy, 0.0)
        return carry

    lax.fori_loop(0, own_blocks, atoms, 0)

    lane_row = lax.broadcasted_iota(jnp.int32, (1, CH), 1)
    parity = (lane_row >= BLOCK).astype(F32)

    def backward(e, carry):
        build_terms(e, feats, weights, terms, terms0)
        odd = lax.broadcasted_iota(jnp.int32, (CHUNK, CH), 1) >= BLOCK
        for row0 in range(0, width, CHUNK):
            dx, dy, dz, x2, y2, z2, s, t, t2 = geometry(e, row0, pos_i, pos_j, keep)
            env = t2 * t
            denv = -3.0 * t2
            ys = harmonics(dx, dy, dz, x2, y2, z2)
            u = jnp.minimum(s, 1.0) - 0.5
            c1 = -sin_pi(u)
            s1 = cos_pi(u)
            c2 = 2.0 * c1 * c1 - 1.0
            s2 = 2.0 * c1 * s1
            two_c2 = 2.0 * c2
            c_before, c_now = jnp.where(odd, c1, c2), jnp.where(odd, c1, 1.0)
            s_before, s_now = jnp.where(odd, -s1, -s2), jnp.where(odd, s1, 0.0)
            rows = slice(row0, row0 + CHUNK)
            for m in range(4):
                sl = slice(m * CH, (m + 1) * CH)
                order = math.pi * (2.0 * m + parity)
                rad[rows, sl] = env * c_now
                drad[rows, sl] = denv * c_now - env * (order * s_now)
                c_before, c_now = c_now, two_c2 * c_now - c_before
                s_before, s_now = s_now, two_c2 * s_now - s_before
            for k in range(1, 9):
                harm[k, rows, :] = ys[k]
        centre = pl.ds(pl.multiple_of(e * BLOCK, BLOCK), width)
        grad = mm_t(dmsg[centre, :], terms0[...])
        total = None
        for m in range(4):
            sl = slice(m * CH, (m + 1) * CH)
            part = drad[:, sl] * grad[:, sl]
            total = part if total is None else total + part
        accum[...] = total
        for k in range(1, 9):
            lhs = jnp.concatenate(
                [dmsg[centre, 0:CH], dmsg[centre, k * CH : (k + 1) * CH]], axis=1
            )
            grad = mm_t(lhs, pair_terms(terms, k))
            by_r = None
            by_y = None
            for m in range(4):
                sl = slice(m * CH, (m + 1) * CH)
                part_r = drad[:, sl] * grad[:, sl]
                part_y = rad[:, sl] * grad[:, sl]
                by_r = part_r if by_r is None else by_r + part_r
                by_y = part_y if by_y is None else by_y + part_y
            accum[...] += harm[k] * by_r
            gharm[k] = by_y
        tot = [jnp.zeros((CHUNK, CH), F32) for _ in range(3)]
        lane = lax.broadcasted_iota(jnp.int32, (CHUNK, CH), 1)
        for row0 in range(0, width, CHUNK):
            rows = slice(row0, row0 + CHUNK)
            dx, dy, dz = (harm[k, rows, :] for k in (1, 2, 3))
            gy = [None] + [gharm[k, rows, :] for k in range(1, 9)]
            radial = 2.0 * accum[rows, :]
            gx = dx * (radial - gy[6]) + gy[1] + ROOT_THREE * (dy * gy[4] + dz * gy[7] + dx * gy[8])
            gyy = dy * (radial - gy[6]) + gy[2] + ROOT_THREE * (dx * gy[4] + dz * gy[5] - dy * gy[8])
            gz = dz * (radial + 2.0 * gy[6]) + gy[3] + ROOT_THREE * (dy * gy[5] + dx * gy[7])
            parts = (gx, gyy, gz)
            tot = [a + b for a, b in zip(tot, parts)]
            sums = [jnp.sum(p, axis=1, keepdims=True) for p in parts]
            add = jnp.where(lane == 0, sums[0], jnp.where(lane == 1, sums[1], jnp.where(lane == 2, sums[2], 0.0)))
            at = pl.ds(pl.multiple_of(e * BLOCK + row0, CHUNK), CHUNK)
            cols[at, :] += add
        sub = lax.broadcasted_iota(jnp.int32, (8, CH), 0)
        col_sums = [jnp.sum(p, axis=0, keepdims=True) for p in tot]
        nbr_out[e] = jnp.where(
            sub == 0, col_sums[0], jnp.where(sub == 1, col_sums[1], jnp.where(sub == 2, col_sums[2], 0.0))
        )
        return carry

    lax.fori_loop(0, ext_blocks, backward, 0)
    cols_out[...] = jnp.transpose(cols[...])[0:8, :]


def block_stage(keep, count, pos_i, pos_j, feats, gains, weights, mix, self_w, readout):
    ext_blocks = pos_j.shape[0]
    own_rows = (ext_blocks - 2) * BLOCK
    pad_rows = pos_i.shape[0]
    vmem = pl.BlockSpec(memory_space=pltpu.VMEM)
    smem = pl.BlockSpec(memory_space=pltpu.SMEM)
    width = 3 * BLOCK
    return pl.pallas_call(
        block_kernel,
        out_shape=(
            jax.ShapeDtypeStruct((8, pad_rows), F32),
            jax.ShapeDtypeStruct((ext_blocks, 8, CH), F32),
            jax.ShapeDtypeStruct((own_rows, CH), BF16),
        ),
        in_specs=[smem, smem] + [vmem] * 8,
        out_specs=(vmem, vmem, vmem),
        scratch_shapes=[
            pltpu.VMEM((9, width, NB * BLOCK), BF16),
            pltpu.VMEM((NB * BLOCK, 10 * CH), BF16),
            pltpu.VMEM((NB * BLOCK, 9 * CH), BF16),
            pltpu.VMEM((9, pad_rows, CH), F32),
            pltpu.VMEM((pad_rows, 9 * CH), BF16),
            pltpu.VMEM((width, NB * BLOCK), F32),
            pltpu.VMEM((width, NB * BLOCK), F32),
            pltpu.VMEM((9, width, CH), F32),
            pltpu.VMEM((9, width, CH), F32),
            pltpu.VMEM((width, CH), F32),
            pltpu.VMEM((pad_rows, CH), F32),
        ],
        compiler_params=pltpu.CompilerParams(vmem_limit_bytes=50 * 1024 * 1024),
        name="block_stage",
    )(keep, count, pos_i, pos_j, feats, gains, weights, mix, self_w, readout)


def gather_kernel(arrival, count, rows_in, out):
    atom_rows = arrival.shape[0]
    source = rows_in.shape[0]
    index = arrival[...]
    slot = (index // 6) * 8 + index % 6
    lane = lax.broadcasted_iota(jnp.int32, (atom_rows, source), 1)
    pick = jnp.where(slot == lane, count[...], 0.0).astype(BF16)
    for k in range(9):
        out[:, k * CH : (k + 1) * CH] = mm(pick, rows_in[:, k * CH : (k + 1) * CH]).astype(BF16)


def gather_stage(arrival, live, rows_in):
    atom_rows = arrival.shape[0]
    vmem = pl.BlockSpec(memory_space=pltpu.VMEM)
    return pl.pallas_call(
        gather_kernel,
        out_shape=jax.ShapeDtypeStruct((atom_rows, rows_in.shape[1]), BF16),
        in_specs=[vmem] * 3,
        out_specs=vmem,
        compiler_params=pltpu.CompilerParams(vmem_limit_bytes=32 * 1024 * 1024),
        name="gather_stage",
    )(arrival, live, rows_in)


def ring_pairs(axes):
    count = math.prod(lax.axis_size(axis) for axis in axes)
    forward = [(i, i + 1) for i in range(count - 1)]
    backward = [(target, source) for source, target in forward]
    return forward, backward


def per_device(
    features_domain,
    arrival,
    positions,
    species,
    block_count,
    pair_block,
    radial_weights,
    species_weights,
    mix_weight,
    self_weight,
    readout,
):
    axes = ("dom", "blk")
    devices = lax.axis_size(axes)
    atom_rows, feature_cols = features_domain.shape
    piece = atom_rows // devices
    blocks = atom_rows // BLOCK
    forward, backward = ring_pairs(axes)

    parcels = jnp.pad(
        features_domain.reshape(devices, piece, feature_cols), ((0, 0), (0, 8 - piece), (0, 0))
    )
    received = lax.all_to_all(parcels, axes, split_axis=0, concat_axis=0, tiled=True)
    received = received.reshape(devices * 8, feature_cols)

    coords = positions.T
    low = lax.ppermute(coords[:, atom_rows - BLOCK :], axes, forward)
    high = lax.ppermute(coords[:, :BLOCK], axes, backward)
    coords_ext = jnp.concatenate([low, coords, high], axis=1)
    pos_i = jnp.pad(coords_ext, ((0, 5), (BLOCK, BLOCK))).T
    by_block = coords_ext.reshape(3, blocks + 2, BLOCK).transpose(1, 0, 2)
    pos_j = jnp.pad(jnp.concatenate([by_block, by_block], axis=2), ((0, 0), (0, 5), (0, 0)))
    listed = jnp.pad((pair_block >= 0).astype(F32), ((2, 2), (0, 0)))
    keep = jnp.stack(
        [listed[0 : blocks + 2, 2], listed[1 : blocks + 3, 1], listed[2 : blocks + 4, 0]], axis=1
    ).reshape(-1)
    live = (jnp.arange(BLOCK, dtype=jnp.int32)[None, :] < block_count[:, None]).astype(F32)
    total = species_weights.shape[0]
    one_hot = (species[:, None] == jnp.arange(total, dtype=jnp.int32)[None, :]).astype(F32)
    gains = jnp.dot(one_hot, species_weights.reshape(total, -1), precision=lax.Precision.HIGHEST)

    relaid = gather_stage(arrival[:, None], live.reshape(atom_rows, 1), received)
    below = lax.ppermute(relaid[atom_rows - BLOCK :], axes, forward)
    above = lax.ppermute(relaid[:BLOCK], axes, backward)
    feats = jnp.concatenate([below, relaid, above], axis=0)

    cols, nbr, new_rows = block_stage(
        keep,
        block_count,
        pos_i,
        pos_j,
        feats,
        gains,
        radial_weights,
        mix_weight,
        self_weight,
        readout[None, :],
    )
    energies = cols[3, 2 * BLOCK : 2 * BLOCK + atom_rows]
    on_nbr = nbr[:, 0:3, :BLOCK] + nbr[:, 0:3, BLOCK:]
    from_low = lax.ppermute(on_nbr[blocks + 1], axes, forward)
    from_high = lax.ppermute(on_nbr[0], axes, backward)
    own = on_nbr[1 : blocks + 1]
    own = own.at[0].add(from_low).at[blocks - 1].add(from_high)
    own = own.transpose(1, 0, 2).reshape(3, atom_rows)
    forces = (cols[0:3, 2 * BLOCK : 2 * BLOCK + atom_rows] - own).T
    return (energies, forces, new_rows)


def solution(mesh):
    placed = (
        P(("dom", "blk"), None),
        P(("dom", "blk")),
        P(("dom", "blk"), None),
        P(("dom", "blk")),
        P(("dom", "blk")),
        P(("dom", "blk"), None),
        P(),
        P(),
        P(),
        P(),
        P(),
    )
    return jax.shard_map(
        per_device,
        mesh=mesh,
        in_specs=placed,
        out_specs=(P(("dom", "blk")), P(("dom", "blk"), None), P(("dom", "blk"), None)),
        check_vma=False,
    )
```

```python
import functools
import math

import jax
import jax.numpy as jnp
import numpy as np
from jax import lax
from jax.experimental import pallas as pl
from jax.experimental.pallas import tpu as pltpu
from jax.sharding import PartitionSpec as P

BLOCK = 64
CH = 128
ROOT_THREE = math.sqrt(3.0)
DOT_PATH = (0, 5, 5, 5, 6, 6, 6, 6, 6)
CARRY_PATH = (-1, 3, 3, 3, 4, 4, 4, 4, 4)
LIFT_PATH = (-1, 1, 1, 1, 2, 2, 2, 2, 2)
CHUNK = 16
NB = 8
F32 = jnp.float32
BF16 = jnp.bfloat16


def mm(a, b):
    return jnp.dot(a, b, preferred_element_type=F32)


def mm_t(a, b):
    return lax.dot_general(a, b, (((1,), (1,)), ((), ())), preferred_element_type=F32)


def sin_pi(u):
    u2 = u * u
    acc = jnp.full_like(u, -(math.pi**11) / math.factorial(11))
    for power in (9, 7, 5, 3, 1):
        sign = 1.0 if power % 4 == 1 else -1.0
        acc = acc * u2 + sign * math.pi**power / math.factorial(power)
    return acc * u


def cos_pi(u):
    u2 = u * u
    acc = jnp.full_like(u, math.pi**12 / math.factorial(12))
    for power in (10, 8, 6, 4, 2, 0):
        sign = 1.0 if power % 4 == 0 else -1.0
        acc = acc * u2 + sign * math.pi**power / math.factorial(power)
    return acc


def harmonics(dx, dy, dz, x2, y2, z2):
    return (
        None,
        dx,
        dy,
        dz,
        ROOT_THREE * (dx * dy),
        ROOT_THREE * (dy * dz),
        z2 - 0.5 * (x2 + y2),
        ROOT_THREE * (dz * dx),
        (0.5 * ROOT_THREE) * (x2 - y2),
    )


def geometry(e, row0, pos_i, pos_j, keep):
    start = pl.multiple_of(e * BLOCK + row0, CHUNK)
    centre = pos_i[pl.ds(start, CHUNK), :]
    nbr = pos_j[e]
    dx = nbr[0:1, :] - centre[:, 0:1]
    dy = nbr[1:2, :] - centre[:, 1:2]
    dz = nbr[2:3, :] - centre[:, 2:3]
    x2, y2, z2 = dx * dx, dy * dy, dz * dz
    return dx, dy, dz, x2, y2, z2


def edge_tasks(e, low, width, pos_i, pos_j, keep, put_edge, put_slope):
    def task(row0):
        odd = lax.broadcasted_iota(jnp.int32, (CHUNK, CH), 1) >= BLOCK
        parity = odd.astype(F32)
        dx, dy, dz, x2, y2, z2 = geometry(e, row0, pos_i, pos_j, keep)
        s = x2 + y2 + z2
        t = jnp.maximum(1.0 - s, 0.0)
        t2 = t * t * keep[e * 3 + row0 // BLOCK]
        if row0 // BLOCK == 1:
            row = lax.broadcasted_iota(jnp.int32, (CHUNK, CH), 0) + row0 % BLOCK
            col = lax.broadcasted_iota(jnp.int32, (CHUNK, CH), 1) % BLOCK
            t2 = jnp.where(row == col, 0.0, t2)
        env = t2 * t
        denv = -3.0 * t2
        ys = harmonics(dx, dy, dz, x2, y2, z2)
        u = jnp.minimum(s, 1.0) - 0.5
        c1 = -sin_pi(u)
        s1 = cos_pi(u)
        c2 = 2.0 * c1 * c1 - 1.0
        s2 = 2.0 * c1 * s1
        two_c2 = 2.0 * c2
        c_before, c_now = jnp.where(odd, c1, c2), jnp.where(odd, c1, 1.0)
        s_before, s_now = jnp.where(odd, -s1, -s2), jnp.where(odd, s1, 0.0)
        rows = slice(row0 - low, row0 - low + CHUNK)
        ys = [None] + [y.astype(BF16) for y in ys[1:]]
        for m in range(4):
            cols = slice(m * CH, (m + 1) * CH)
            radial = (env * c_now).astype(BF16)
            order = math.pi * (2.0 * m + parity)
            put_slope(rows, cols, (denv * c_now - env * (order * s_now)).astype(BF16))
            put_edge(0, rows, cols, radial)
            for k in range(1, 9):
                put_edge(k, rows, cols, radial * ys[k])
            c_before, c_now = c_now, two_c2 * c_now - c_before
            s_before, s_now = s_now, two_c2 * s_now - s_before

    return [functools.partial(task, row0) for row0 in range(low, low + width, CHUNK)]


def mingle(main, *others):
    main = list(main)
    queue = [unit for other in others for unit in other]
    done = 0
    for position, step in enumerate(main):
        step()
        upto = len(queue) * (position + 1) // len(main)
        while done < upto:
            queue[done]()
            done += 1


def term_tasks(e, feats, weights, terms, terms0):
    def task(row0, k):
        start = pl.multiple_of(e * BLOCK + row0, CHUNK)
        hk = feats[pl.ds(start, CHUNK), k * CH : (k + 1) * CH]
        for n in range(NB):
            rows = slice(n * BLOCK + row0, n * BLOCK + row0 + CHUNK)
            if k == 0:
                terms0[rows, 0:CH] = hk * weights[n, 0:1, :]
                for q in range(2):
                    terms[rows, (8 + q) * CH : (9 + q) * CH] = hk * weights[n, 1 + q : 2 + q, :]
            else:
                dot_w = weights[n, DOT_PATH[k] : DOT_PATH[k] + 1, :]
                carry_w = weights[n, CARRY_PATH[k] : CARRY_PATH[k] + 1, :]
                terms[rows, (k - 1) * CH : k * CH] = hk * dot_w
                terms0[rows, k * CH : (k + 1) * CH] = hk * carry_w

    return [functools.partial(task, row0, k) for k in range(9) for row0 in range(0, BLOCK, CHUNK)]


def pair_terms(terms, k):
    q = LIFT_PATH[k] - 1
    return jnp.concatenate(
        [terms[:, (k - 1) * CH : k * CH], terms[:, (8 + q) * CH : (9 + q) * CH]], axis=1
    )


def message_tasks(e, low, width, edges, terms, terms0, msg):
    rows = pl.ds(pl.multiple_of(e * BLOCK + low, BLOCK), width)

    def scalar():
        msg[0, rows, :] += mm(edges[0], terms0[:, 0:CH])

    def carried(k):
        both = mm(edges[0], terms0[:, k * CH : (k + 2) * CH])
        msg[k, rows, :] += both[:, 0:CH]
        msg[k + 1, rows, :] += both[:, CH:]

    def paired(k):
        both = mm(edges[k], pair_terms(terms, k))
        msg[0, rows, :] += both[:, 0:CH]
        msg[k, rows, :] += both[:, CH:]

    return (
        [scalar]
        + [functools.partial(carried, k) for k in range(1, 9, 2)]
        + [functools.partial(paired, k) for k in range(1, 9)]
    )


def pull_tasks(e, low, width, radial, slope, terms, terms0, dmsg, by_r, by_y):
    centre = pl.ds(pl.multiple_of(e * BLOCK + low, BLOCK), width)

    def first():
        grad = mm_t(dmsg[centre, :], terms0[...]).astype(BF16)
        total = None
        for m in range(4):
            sl = slice(m * CH, (m + 1) * CH)
            part = slope[:, sl] * grad[:, sl]
            total = part if total is None else total + part
        by_r[0, 0:width, :] = total

    def order(k):
        lhs = jnp.concatenate([dmsg[centre, 0:CH], dmsg[centre, k * CH : (k + 1) * CH]], axis=1)
        grad = mm_t(lhs, pair_terms(terms, k)).astype(BF16)
        total_r = None
        total_y = None
        for m in range(4):
            sl = slice(m * CH, (m + 1) * CH)
            part_r = slope[:, sl] * grad[:, sl]
            part_y = radial[:, sl] * grad[:, sl]
            total_r = part_r if total_r is None else total_r + part_r
            total_y = part_y if total_y is None else total_y + part_y
        by_r[k, 0:width, :] = total_r
        by_y[k, 0:width, :] = total_y

    return [first] + [functools.partial(order, k) for k in range(1, 9)]


def force_tasks(e, low, width, by_r, by_y, pos_i, pos_j, keep, cols, nbr_out):
    state = {"tot": [jnp.zeros((CHUNK, CH), F32) for _ in range(3)]}
    lane = lax.broadcasted_iota(jnp.int32, (CHUNK, CH), 1)

    def task(row0):
        rows = slice(row0 - low, row0 - low + CHUNK)
        dx, dy, dz, x2, y2, z2 = geometry(e, row0, pos_i, pos_j, keep)
        ys = harmonics(dx, dy, dz, x2, y2, z2)
        radial_sum = by_r[0, rows, :].astype(F32)
        for k in range(1, 9):
            radial_sum += ys[k] * by_r[k, rows, :].astype(F32)
        radial_sum *= 2.0
        gy = [None] + [by_y[k, rows, :].astype(F32) for k in range(1, 9)]
        along = radial_sum - gy[6]
        parts = (
            dx * along + gy[1] + ROOT_THREE * (dy * gy[4] + dz * gy[7] + dx * gy[8]),
            dy * along + gy[2] + ROOT_THREE * (dx * gy[4] + dz * gy[5] - dy * gy[8]),
            dz * (radial_sum + 2.0 * gy[6]) + gy[3] + ROOT_THREE * (dy * gy[5] + dx * gy[7]),
        )
        state["tot"] = [a + b for a, b in zip(state["tot"], parts)]
        sums = [jnp.sum(p, axis=1, keepdims=True) for p in parts]
        add = jnp.where(
            lane == 0, sums[0], jnp.where(lane == 1, sums[1], jnp.where(lane == 2, sums[2], 0.0))
        )
        at = pl.ds(pl.multiple_of(e * BLOCK + row0, CHUNK), CHUNK)
        cols[at, :] += add

    def finish():
        sub = lax.broadcasted_iota(jnp.int32, (8, CH), 0)
        sums = [jnp.sum(p, axis=0, keepdims=True) for p in state["tot"]]
        nbr_out[e] = jnp.where(
            sub == 0, sums[0], jnp.where(sub == 1, sums[1], jnp.where(sub == 2, sums[2], 0.0))
        )

    return [functools.partial(task, row0) for row0 in range(low, low + width, CHUNK)] + [finish]


def block_kernel(
    keep,
    count,
    arrival,
    live_in,
    received,
    pos_i,
    pos_j,
    gains,
    weights_in,
    mix,
    self_w,
    readout,
    force_out,
    energy_out,
    new_out,
    pick,
    feats,
    nbr_out,
    inbox,
    edges_a,
    edges_b,
    rad_all,
    slope_all,
    terms_a,
    terms_b,
    first_a,
    first_b,
    edges_h,
    slopes_h,
    msg,
    dmsg,
    by_r_a,
    by_r_b,
    by_y_a,
    by_y_b,
    cols,
    weights,
    send_sems,
    recv_sems,
):
    own_blocks = pos_j.shape[0] - 2
    width = 3 * BLOCK
    weights[...] = weights_in[...].astype(BF16)
    inner = lax.axis_size("blk")
    ranks = lax.axis_size("dom") * inner
    me = lax.axis_index("dom") * inner + lax.axis_index("blk")

    def place(rank):
        return (rank // inner, lax.rem(rank, inner))

    after = place(lax.rem(me + 1, ranks))
    before = place(lax.rem(me + ranks - 1, ranks))

    def send(source, target, lane, device):
        return pltpu.make_async_remote_copy(
            src_ref=source,
            dst_ref=target,
            send_sem=send_sems.at[lane],
            recv_sem=recv_sems.at[lane],
            device_id=device,
            device_id_type=pl.DeviceIdType.MESH,
        )

    barrier = pltpu.get_barrier_semaphore()
    for device in (before, after):
        pl.semaphore_signal(barrier, inc=1, device_id=device, device_id_type=pl.DeviceIdType.MESH)

    rows_own = own_blocks * BLOCK
    index = arrival[...]
    slot_of = (index // 6) * 8 + index % 6
    alive = live_in[...]
    for tile in range(received.shape[0] // CH):
        lane_id = lax.broadcasted_iota(jnp.int32, (rows_own, CH), 1) + tile * CH
        pick[:, tile * CH : (tile + 1) * CH] = jnp.where(slot_of == lane_id, alive, 0.0).astype(BF16)
    for low in range(0, 9 * CH, 2 * CH):
        high = min(low + 2 * CH, 9 * CH)
        feats[BLOCK : BLOCK + rows_own, low:high] = mm(pick[...], received[:, low:high]).astype(BF16)

    pl.semaphore_wait(barrier, 2)
    to_before = send(feats.at[BLOCK : 2 * BLOCK], feats.at[BLOCK + rows_own : 2 * BLOCK + rows_own], 0, before)
    to_after = send(feats.at[rows_own : BLOCK + rows_own], feats.at[0:BLOCK], 1, after)
    to_before.start()
    to_after.start()
    edge_bufs = (edges_a, edges_b)
    term_bufs, first_bufs = (terms_a, terms_b), (first_a, first_b)
    sums_bufs = ((by_r_a, by_y_a), (by_r_b, by_y_b))

    def own_edges(b, buf):
        def put_edge(k, rows, cols_, value):
            buf[k, rows, cols_] = value
            if k == 0:
                rad_all[b, rows, cols_] = value

        def put_slope(rows, cols_, value):
            slope_all[b, rows, cols_] = value

        return edge_tasks(b + 1, 0, width, pos_i, pos_j, keep, put_edge, put_slope)

    msg[...] = jnp.zeros_like(msg)
    cols[...] = jnp.zeros_like(cols)
    dmsg[...] = jnp.zeros_like(dmsg)
    last = own_blocks - 1
    mingle(own_edges(0, edges_a), term_tasks(1, feats, weights, terms_a, first_a))

    def forward(i, carry):
        for half in range(2):
            b = i * 2 + half
            ahead = jnp.minimum(b + 1, last)
            mingle(
                message_tasks(b + 1, 0, width, edge_bufs[half], term_bufs[half], first_bufs[half], msg),
                own_edges(ahead, edge_bufs[1 - half]),
                term_tasks(ahead + 1, feats, weights, term_bufs[1 - half], first_bufs[1 - half]),
            )
        return carry

    lax.fori_loop(0, own_blocks // 2, forward, 0)

    to_before.wait()
    to_after.wait()
    halo = ((0, 2 * BLOCK), (own_blocks + 1, 0))
    for side, (e, low) in enumerate(halo):
        def put_edge(k, rows, cols_, value):
            edges_h[side, k, rows, cols_] = value

        def put_slope(rows, cols_, value):
            slopes_h[side, rows, cols_] = value

        mingle(
            edge_tasks(e, low, BLOCK, pos_i, pos_j, keep, put_edge, put_slope),
            term_tasks(e, feats, weights, term_bufs[side], first_bufs[side]),
        )
    for side, (e, low) in enumerate(halo):
        mingle(
            message_tasks(e, low, BLOCK, edges_h.at[side], term_bufs[side], first_bufs[side], msg)
        )

    size = 2 * BLOCK

    def atoms(i, carry):
        rows = pl.ds(pl.multiple_of(i * size + 2 * BLOCK, size), size)
        own = pl.ds(pl.multiple_of(i * size, size), size)
        ext = pl.ds(pl.multiple_of(i * size + BLOCK, BLOCK), size)
        slot = lax.broadcasted_iota(jnp.int32, (BLOCK, 1), 0)
        live = jnp.concatenate(
            [(slot < count[2 * i + step]).astype(F32) for step in range(2)], axis=0
        )
        m = [msg[k, rows, :] for k in range(9)]
        first = m[1] * m[1] + m[2] * m[2] + m[3] * m[3]
        second = m[4] * m[4] + m[5] * m[5] + m[6] * m[6] + m[7] * m[7] + m[8] * m[8]
        g0, g1, g2 = (gains[own, l * CH : (l + 1) * CH] for l in range(3))
        basis = m[0] + g0 * (m[0] * m[0]) + g1 * first + g2 * second
        mixed = mm(basis.astype(BF16), mix[...]) + mm(feats[ext, 0:CH], self_w[...])
        new_out[own, :] = (mixed * live).astype(BF16)
        gate = 1.0 / (1.0 + jnp.exp(-mixed))
        value = mixed * gate
        energy = live * jnp.sum(readout[...] * value, axis=1, keepdims=True)
        slope = live * readout[...] * (gate + value * (1.0 - gate))
        dbasis = mm_t(slope.astype(BF16), mix[...]).astype(BF16).astype(F32)
        dmsg[rows, 0:CH] = (dbasis * (1.0 + 2.0 * g0 * m[0])).astype(BF16)
        for k in range(1, 9):
            gain = g1 if k < 4 else g2
            dmsg[rows, k * CH : (k + 1) * CH] = (2.0 * dbasis * gain * m[k]).astype(BF16)
        lane = lax.broadcasted_iota(jnp.int32, (size, CH), 1)
        cols[rows, :] = jnp.where(lane == 3, energy, 0.0)
        return carry

    lax.fori_loop(0, own_blocks // 2, atoms, 0)

    for side, (e, low) in enumerate(halo):
        mingle(
            pull_tasks(
                e, low, BLOCK, edges_h.at[side, 0], slopes_h.at[side], term_bufs[side],
                first_bufs[side], dmsg, *sums_bufs[side],
            )
        )
    for side, (e, low) in enumerate(halo):
        mingle(force_tasks(e, low, BLOCK, *sums_bufs[side], pos_i, pos_j, keep, cols, nbr_out))
    force_before = send(nbr_out.at[0], inbox.at[0], 2, before)
    force_after = send(nbr_out.at[own_blocks + 1], inbox.at[1], 3, after)
    force_before.start()
    force_after.start()
    mingle(term_tasks(1, feats, weights, terms_a, first_a))

    def pull(b, half):
        return pull_tasks(
            b + 1, 0, width, rad_all.at[b], slope_all.at[b], term_bufs[half], first_bufs[half],
            dmsg, *sums_bufs[half],
        )

    def ahead_terms(b, half):
        return term_tasks(b + 1, feats, weights, term_bufs[half], first_bufs[half])

    def force(b, half):
        return force_tasks(
            b + 1, 0, width, *sums_bufs[half], pos_i, pos_j, keep, cols, nbr_out
        )

    mingle(pull(0, 0), ahead_terms(1, 1))

    def backward(i, carry):
        b = i * 2 + 1
        mingle(pull(b, 1), force(b - 1, 0), ahead_terms(b + 1, 0))
        mingle(pull(b + 1, 0), force(b, 1), ahead_terms(jnp.minimum(b + 2, last), 1))
        return carry

    lax.fori_loop(0, own_blocks // 2 - 1, backward, 0)
    mingle(pull(last, 1), force(last - 1, 0))
    mingle(force(last, 1))
    force_before.wait()
    force_after.wait()
    nbr_out[1] += inbox[1]
    nbr_out[own_blocks] += inbox[0]
    half_lane = lax.broadcasted_iota(jnp.int32, (8, CH), 1) < BLOCK
    for i in range(own_blocks // 2):
        lanes = slice(i * CH, (i + 1) * CH)
        flat = jnp.transpose(cols[2 * BLOCK + i * CH : 2 * BLOCK + (i + 1) * CH, :])[0:8, :]
        even, odd_ = nbr_out[2 * i + 1], nbr_out[2 * i + 2]
        even = even + pltpu.roll(even, BLOCK, 1)
        odd_ = odd_ + pltpu.roll(odd_, BLOCK, 1)
        total = flat - jnp.where(half_lane, even, odd_)
        force_out[:, lanes] = total[0:3, :]
        energy_out[:, lanes] = total[3:4, :]


def block_stage(
    keep, count, arrival, live, received, pos_i, pos_j, gains, weights, mix, self_w, readout
):
    ext_blocks = pos_j.shape[0]
    own_rows = (ext_blocks - 2) * BLOCK
    pad_rows = pos_i.shape[0]
    vmem = pl.BlockSpec(memory_space=pltpu.VMEM)
    smem = pl.BlockSpec(memory_space=pltpu.SMEM)
    width, depth = 3 * BLOCK, NB * BLOCK
    return pl.pallas_call(
        block_kernel,
        out_shape=(
            jax.ShapeDtypeStruct((3, own_rows), F32),
            jax.ShapeDtypeStruct((1, own_rows), F32),
            jax.ShapeDtypeStruct((own_rows, CH), BF16),
        ),
        in_specs=[smem, smem] + [vmem] * 10,
        out_specs=(vmem, vmem, vmem),
        scratch_shapes=[
            pltpu.VMEM((own_rows, received.shape[0]), BF16),
            pltpu.VMEM((own_rows + 2 * BLOCK, 9 * CH), BF16),
            pltpu.VMEM((ext_blocks, 8, CH), F32),
            pltpu.VMEM((2, 8, CH), F32),
            pltpu.VMEM((9, width, depth), BF16),
            pltpu.VMEM((9, width, depth), BF16),
            pltpu.VMEM((ext_blocks - 2, width, depth), BF16),
            pltpu.VMEM((ext_blocks - 2, width, depth), BF16),
            pltpu.VMEM((depth, 10 * CH), BF16),
            pltpu.VMEM((depth, 10 * CH), BF16),
            pltpu.VMEM((depth, 9 * CH), BF16),
            pltpu.VMEM((depth, 9 * CH), BF16),
            pltpu.VMEM((2, 9, BLOCK, depth), BF16),
            pltpu.VMEM((2, BLOCK, depth), BF16),
            pltpu.VMEM((9, pad_rows, CH), F32),
            pltpu.VMEM((pad_rows, 9 * CH), BF16),
            pltpu.VMEM((9, width, CH), BF16),
            pltpu.VMEM((9, width, CH), BF16),
            pltpu.VMEM((9, width, CH), BF16),
            pltpu.VMEM((9, width, CH), BF16),
            pltpu.VMEM((pad_rows, CH), F32),
            pltpu.VMEM((NB, 7, CH), BF16),
            pltpu.SemaphoreType.DMA((4,)),
            pltpu.SemaphoreType.DMA((4,)),
        ],
        compiler_params=pltpu.CompilerParams(
            vmem_limit_bytes=50 * 1024 * 1024, collective_id=0, has_side_effects=True
        ),
        name="block_stage",
    )(keep, count, arrival, live, received, pos_i, pos_j, gains, weights, mix, self_w, readout)


def ring_pairs(axes):
    count = math.prod(lax.axis_size(axis) for axis in axes)
    forward = [(i, i + 1) for i in range(count - 1)]
    backward = [(target, source) for source, target in forward]
    return forward, backward


def per_device(
    features_domain,
    arrival,
    positions,
    species,
    block_count,
    pair_block,
    radial_weights,
    species_weights,
    mix_weight,
    self_weight,
    readout,
):
    axes = ("dom", "blk")
    devices = lax.axis_size(axes)
    atom_rows, feature_cols = features_domain.shape
    piece = atom_rows // devices
    blocks = atom_rows // BLOCK
    forward, backward = ring_pairs(axes)

    parcels = jnp.pad(
        features_domain.reshape(devices, piece, feature_cols), ((0, 0), (0, 8 - piece), (0, 0))
    )
    received = lax.all_to_all(parcels, axes, split_axis=0, concat_axis=0, tiled=True)
    received = received.reshape(devices * 8, feature_cols)

    coords = positions.T
    low = lax.ppermute(coords[:, atom_rows - BLOCK :], axes, forward)
    high = lax.ppermute(coords[:, :BLOCK], axes, backward)
    coords_ext = jnp.concatenate([low, coords, high], axis=1)
    pos_i = jnp.pad(coords_ext, ((0, 5), (BLOCK, BLOCK))).T
    by_block = coords_ext.reshape(3, blocks + 2, BLOCK).transpose(1, 0, 2)
    pos_j = jnp.pad(jnp.concatenate([by_block, by_block], axis=2), ((0, 0), (0, 5), (0, 0)))
    listed = jnp.pad((pair_block >= 0).astype(F32), ((2, 2), (0, 0)))
    keep = jnp.stack(
        [listed[0 : blocks + 2, 2], listed[1 : blocks + 3, 1], listed[2 : blocks + 4, 0]], axis=1
    ).reshape(-1)
    live = (jnp.arange(BLOCK, dtype=jnp.int32)[None, :] < block_count[:, None]).astype(F32)
    total = species_weights.shape[0]
    one_hot = (species[:, None] == jnp.arange(total, dtype=jnp.int32)[None, :]).astype(F32)
    gains = jnp.dot(one_hot, species_weights.reshape(total, -1), precision=lax.Precision.HIGHEST)

    forces, energies, new_rows = block_stage(
        keep,
        block_count,
        arrival[:, None],
        live.reshape(atom_rows, 1),
        received,
        pos_i,
        pos_j,
        gains,
        radial_weights,
        mix_weight,
        self_weight,
        readout[None, :],
    )
    return (energies.reshape(atom_rows), forces.T, new_rows)


def solution(mesh):
    placed = (
        P(("dom", "blk"), None),
        P(("dom", "blk")),
        P(("dom", "blk"), None),
        P(("dom", "blk")),
        P(("dom", "blk")),
        P(("dom", "blk"), None),
        P(),
        P(),
        P(),
        P(),
        P(),
    )
    return jax.shard_map(
        per_device,
        mesh=mesh,
        in_specs=placed,
        out_specs=(P(("dom", "blk")), P(("dom", "blk"), None), P(("dom", "blk"), None)),
        check_vma=False,
    )
```

```python
import functools
import math

import jax
import jax.numpy as jnp
import numpy as np
from jax import lax
from jax.experimental import pallas as pl
from jax.experimental.pallas import tpu as pltpu
from jax.sharding import PartitionSpec as P

BLOCK = 64
CH = 128
ROOT_THREE = math.sqrt(3.0)
DOT_PATH = (0, 5, 5, 5, 6, 6, 6, 6, 6)
CARRY_PATH = (-1, 3, 3, 3, 4, 4, 4, 4, 4)
LIFT_PATH = (-1, 1, 1, 1, 2, 2, 2, 2, 2)
CHUNK = 16
NB = 8
PIECE = 6
F32 = jnp.float32
BF16 = jnp.bfloat16


def mm(a, b):
    return jnp.dot(a, b, preferred_element_type=F32)


def mm_t(a, b):
    return lax.dot_general(a, b, (((1,), (1,)), ((), ())), preferred_element_type=F32)


def sin_pi(u):
    u2 = u * u
    acc = jnp.full_like(u, -(math.pi**11) / math.factorial(11))
    for power in (9, 7, 5, 3, 1):
        sign = 1.0 if power % 4 == 1 else -1.0
        acc = acc * u2 + sign * math.pi**power / math.factorial(power)
    return acc * u


def cos_pi(u):
    u2 = u * u
    acc = jnp.full_like(u, math.pi**12 / math.factorial(12))
    for power in (10, 8, 6, 4, 2, 0):
        sign = 1.0 if power % 4 == 0 else -1.0
        acc = acc * u2 + sign * math.pi**power / math.factorial(power)
    return acc


def harmonics(dx, dy, dz, x2, y2, z2):
    return (
        None,
        dx,
        dy,
        dz,
        ROOT_THREE * (dx * dy),
        ROOT_THREE * (dy * dz),
        z2 - 0.5 * (x2 + y2),
        ROOT_THREE * (dz * dx),
        (0.5 * ROOT_THREE) * (x2 - y2),
    )


def geometry(e, row0, pos_i, pos_j, keep):
    start = pl.multiple_of(e * BLOCK + row0, CHUNK)
    centre = pos_i[pl.ds(start, CHUNK), :]
    nbr = pos_j[e]
    dx = nbr[0:1, :] - centre[:, 0:1]
    dy = nbr[1:2, :] - centre[:, 1:2]
    dz = nbr[2:3, :] - centre[:, 2:3]
    x2, y2, z2 = dx * dx, dy * dy, dz * dz
    return dx, dy, dz, x2, y2, z2


def edge_tasks(e, low, width, pos_i, pos_j, keep, put_edge, put_slope):
    def task(row0):
        odd = lax.broadcasted_iota(jnp.int32, (CHUNK, CH), 1) >= BLOCK
        parity = odd.astype(F32)
        dx, dy, dz, x2, y2, z2 = geometry(e, row0, pos_i, pos_j, keep)
        s = x2 + y2 + z2
        t = jnp.maximum(1.0 - s, 0.0)
        t2 = t * t * keep[e * 3 + row0 // BLOCK]
        if row0 // BLOCK == 1:
            row = lax.broadcasted_iota(jnp.int32, (CHUNK, CH), 0) + row0 % BLOCK
            col = lax.broadcasted_iota(jnp.int32, (CHUNK, CH), 1) % BLOCK
            t2 = jnp.where(row == col, 0.0, t2)
        env = t2 * t
        denv = -3.0 * t2
        ys = harmonics(dx, dy, dz, x2, y2, z2)
        u = jnp.minimum(s, 1.0) - 0.5
        c1 = -sin_pi(u)
        s1 = cos_pi(u)
        c2 = 2.0 * c1 * c1 - 1.0
        s2 = 2.0 * c1 * s1
        two_c2 = 2.0 * c2
        c_before, c_now = jnp.where(odd, c1, c2), jnp.where(odd, c1, 1.0)
        s_before, s_now = jnp.where(odd, -s1, -s2), jnp.where(odd, s1, 0.0)
        rows = slice(row0 - low, row0 - low + CHUNK)
        ys = [None] + [y.astype(BF16) for y in ys[1:]]
        for m in range(4):
            cols = slice(m * CH, (m + 1) * CH)
            radial = (env * c_now).astype(BF16)
            order = math.pi * (2.0 * m + parity)
            put_slope(rows, cols, (denv * c_now - env * (order * s_now)).astype(BF16))
            put_edge(0, rows, cols, radial)
            for k in range(1, 9):
                put_edge(k, rows, cols, radial * ys[k])
            c_before, c_now = c_now, two_c2 * c_now - c_before
            s_before, s_now = s_now, two_c2 * s_now - s_before

    return [functools.partial(task, row0) for row0 in range(low, low + width, CHUNK)]


def mingle(main, *others):
    main = list(main)
    queue = [unit for other in others for unit in other]
    done = 0
    for position, step in enumerate(main):
        step()
        upto = len(queue) * (position + 1) // len(main)
        while done < upto:
            queue[done]()
            done += 1


def term_tasks(e, feats, weights, terms, terms0):
    def task(row0, k):
        start = pl.multiple_of(e * BLOCK + row0, CHUNK)
        hk = feats[pl.ds(start, CHUNK), k * CH : (k + 1) * CH]
        for n in range(NB):
            rows = slice(n * BLOCK + row0, n * BLOCK + row0 + CHUNK)
            if k == 0:
                terms0[rows, 0:CH] = hk * weights[n, 0:1, :]
                for q in range(2):
                    terms[rows, (8 + q) * CH : (9 + q) * CH] = hk * weights[n, 1 + q : 2 + q, :]
            else:
                dot_w = weights[n, DOT_PATH[k] : DOT_PATH[k] + 1, :]
                carry_w = weights[n, CARRY_PATH[k] : CARRY_PATH[k] + 1, :]
                terms[rows, (k - 1) * CH : k * CH] = hk * dot_w
                terms0[rows, k * CH : (k + 1) * CH] = hk * carry_w

    return [functools.partial(task, row0, k) for k in range(9) for row0 in range(0, BLOCK, CHUNK)]


def pair_terms(terms, k):
    q = LIFT_PATH[k] - 1
    return jnp.concatenate(
        [terms[:, (k - 1) * CH : k * CH], terms[:, (8 + q) * CH : (9 + q) * CH]], axis=1
    )


def message_tasks(e, low, width, edges, terms, terms0, msg):
    rows = pl.ds(pl.multiple_of(e * BLOCK + low, BLOCK), width)

    def scalar():
        msg[0, rows, :] += mm(edges[0], terms0[:, 0:CH])

    def carried(k):
        both = mm(edges[0], terms0[:, k * CH : (k + 2) * CH])
        msg[k, rows, :] += both[:, 0:CH]
        msg[k + 1, rows, :] += both[:, CH:]

    def paired(k):
        both = mm(edges[k], pair_terms(terms, k))
        msg[0, rows, :] += both[:, 0:CH]
        msg[k, rows, :] += both[:, CH:]

    return (
        [scalar]
        + [functools.partial(carried, k) for k in range(1, 9, 2)]
        + [functools.partial(paired, k) for k in range(1, 9)]
    )


def pull_tasks(e, low, width, radial, slope, terms, terms0, dmsg, by_r, by_y):
    centre = pl.ds(pl.multiple_of(e * BLOCK + low, BLOCK), width)

    def first():
        grad = mm_t(dmsg[centre, :], terms0[...]).astype(BF16)
        total = None
        for m in range(4):
            sl = slice(m * CH, (m + 1) * CH)
            part = slope[:, sl] * grad[:, sl]
            total = part if total is None else total + part
        by_r[0, 0:width, :] = total

    def order(k):
        lhs = jnp.concatenate([dmsg[centre, 0:CH], dmsg[centre, k * CH : (k + 1) * CH]], axis=1)
        grad = mm_t(lhs, pair_terms(terms, k)).astype(BF16)
        total_r = None
        total_y = None
        for m in range(4):
            sl = slice(m * CH, (m + 1) * CH)
            part_r = slope[:, sl] * grad[:, sl]
            part_y = radial[:, sl] * grad[:, sl]
            total_r = part_r if total_r is None else total_r + part_r
            total_y = part_y if total_y is None else total_y + part_y
        by_r[k, 0:width, :] = total_r
        by_y[k, 0:width, :] = total_y

    return [first] + [functools.partial(order, k) for k in range(1, 9)]


def force_tasks(e, low, width, by_r, by_y, pos_i, pos_j, keep, cols, nbr_out):
    state = {"tot": [jnp.zeros((CHUNK, CH), F32) for _ in range(3)]}
    lane = lax.broadcasted_iota(jnp.int32, (CHUNK, CH), 1)

    def task(row0):
        rows = slice(row0 - low, row0 - low + CHUNK)
        dx, dy, dz, x2, y2, z2 = geometry(e, row0, pos_i, pos_j, keep)
        ys = harmonics(dx, dy, dz, x2, y2, z2)
        radial_sum = by_r[0, rows, :].astype(F32)
        for k in range(1, 9):
            radial_sum += ys[k] * by_r[k, rows, :].astype(F32)
        radial_sum *= 2.0
        gy = [None] + [by_y[k, rows, :].astype(F32) for k in range(1, 9)]
        along = radial_sum - gy[6]
        parts = (
            dx * along + gy[1] + ROOT_THREE * (dy * gy[4] + dz * gy[7] + dx * gy[8]),
            dy * along + gy[2] + ROOT_THREE * (dx * gy[4] + dz * gy[5] - dy * gy[8]),
            dz * (radial_sum + 2.0 * gy[6]) + gy[3] + ROOT_THREE * (dy * gy[5] + dx * gy[7]),
        )
        state["tot"] = [a + b for a, b in zip(state["tot"], parts)]
        sums = [jnp.sum(p, axis=1, keepdims=True) for p in parts]
        add = jnp.where(
            lane == 0, sums[0], jnp.where(lane == 1, sums[1], jnp.where(lane == 2, sums[2], 0.0))
        )
        at = pl.ds(pl.multiple_of(e * BLOCK + row0, CHUNK), CHUNK)
        cols[at, :] += add

    def finish():
        sub = lax.broadcasted_iota(jnp.int32, (8, CH), 0)
        sums = [jnp.sum(p, axis=0, keepdims=True) for p in state["tot"]]
        nbr_out[e] = jnp.where(
            sub == 0, sums[0], jnp.where(sub == 1, sums[1], jnp.where(sub == 2, sums[2], 0.0))
        )

    return [functools.partial(task, row0) for row0 in range(low, low + width, CHUNK)] + [finish]


def fill_pick(pick, slot_of, alive, width):
    for tile in range(width // CH):
        lane_id = lax.broadcasted_iota(jnp.int32, (slot_of.shape[0], CH), 1) + tile * CH
        pick[:, tile * CH : (tile + 1) * CH] = jnp.where(slot_of == lane_id, alive, 0.0).astype(BF16)


def pack_kernel(rows_in, out):
    group, source = 256, 256 // 8 * PIECE
    row = lax.broadcasted_iota(jnp.int32, (group, source), 0)
    col = lax.broadcasted_iota(jnp.int32, (group, source), 1)
    parcel, within = row // 8, row % 8
    plain = ((within < PIECE) & (col == parcel * PIECE + within)).astype(F32).astype(BF16)
    last = lax.broadcasted_iota(jnp.int32, (group, CH), 0) % 8 == PIECE + 1
    for t in range(7):
        cols = slice(t * CH, (t + 1) * CH)
        if t < PIECE:
            extra = ((within >= PIECE) & (col == parcel * PIECE + t)).astype(F32).astype(BF16)
        for g in range(out.shape[0] // group):
            at = slice(g * source, (g + 1) * source)
            value = mm(plain, rows_in[at, cols])
            if t < PIECE:
                both = mm(extra, rows_in[at, 7 * CH : 9 * CH])
                value += jnp.where(last, both[:, CH:], both[:, 0:CH])
            out[g * group : (g + 1) * group, cols] = value.astype(BF16)


def pack_stage(rows_in):
    vmem = pl.BlockSpec(memory_space=pltpu.VMEM)
    return pl.pallas_call(
        pack_kernel,
        out_shape=jax.ShapeDtypeStruct((rows_in.shape[0] // PIECE * 8, 7 * CH), BF16),
        in_specs=[vmem],
        out_specs=vmem,
        compiler_params=pltpu.CompilerParams(vmem_limit_bytes=16 * 1024 * 1024),
        name="pack_stage",
    )(rows_in)


def block_kernel(
    keep,
    count,
    arrival,
    live_in,
    received,
    pos_i,
    pos_j,
    gains,
    weights_in,
    mix,
    self_w,
    readout,
    force_out,
    energy_out,
    new_out,
    pick,
    sorted_rows,
    feats,
    nbr_out,
    inbox,
    edges_a,
    edges_b,
    rad_all,
    slope_all,
    terms_a,
    terms_b,
    first_a,
    first_b,
    edges_h,
    slopes_h,
    msg,
    dmsg,
    by_r_a,
    by_r_b,
    by_y_a,
    by_y_b,
    cols,
    weights,
    send_sems,
    recv_sems,
):
    own_blocks = pos_j.shape[0] - 2
    width = 3 * BLOCK
    weights[...] = weights_in[...].astype(BF16)
    inner = lax.axis_size("blk")
    ranks = lax.axis_size("dom") * inner
    me = lax.axis_index("dom") * inner + lax.axis_index("blk")

    def place(rank):
        return (rank // inner, lax.rem(rank, inner))

    after = place(lax.rem(me + 1, ranks))
    before = place(lax.rem(me + ranks - 1, ranks))

    def send(source, target, lane, device):
        return pltpu.make_async_remote_copy(
            src_ref=source,
            dst_ref=target,
            send_sem=send_sems.at[lane],
            recv_sem=recv_sems.at[lane],
            device_id=device,
            device_id_type=pl.DeviceIdType.MESH,
        )

    barrier = pltpu.get_barrier_semaphore()
    for device in (before, after):
        pl.semaphore_signal(barrier, inc=1, device_id=device, device_id_type=pl.DeviceIdType.MESH)

    rows_own = own_blocks * BLOCK
    index = arrival[...]
    parcel = index // PIECE
    within = index - parcel * PIECE
    alive = live_in[...]
    own_feats = slice(BLOCK, BLOCK + rows_own)
    senders = received.shape[0] // 8
    slot_of = within * senders + parcel
    fill_pick(pick, slot_of, alive, PIECE * senders)
    sub_id = lax.broadcasted_iota(jnp.int32, (senders, received.shape[0]), 0)
    row_id = lax.broadcasted_iota(jnp.int32, (senders, received.shape[0]), 1)
    for extra in range(2):
        take = (row_id == sub_id * 8 + (PIECE + extra)).astype(F32).astype(BF16)
        for low in range(0, PIECE * CH, 2 * CH):
            both = mm(take, received[:, low : low + 2 * CH]).astype(BF16)
            for step in range(2):
                r = low // CH + step
                sorted_rows[r * senders : (r + 1) * senders, extra * CH : (extra + 1) * CH] = both[
                    :, step * CH : (step + 1) * CH
                ]
    feats[own_feats, 7 * CH : 9 * CH] = mm(pick[:, 0 : PIECE * senders], sorted_rows[...]).astype(BF16)
    slot_of = parcel * 8 + within
    fill_pick(pick, slot_of, alive, received.shape[0])
    for low in range(0, 7 * CH, 2 * CH):
        high = min(low + 2 * CH, 7 * CH)
        feats[own_feats, low:high] = mm(pick[...], received[:, low:high]).astype(BF16)

    pl.semaphore_wait(barrier, 2)
    to_before = send(feats.at[BLOCK : 2 * BLOCK], feats.at[BLOCK + rows_own : 2 * BLOCK + rows_own], 0, before)
    to_after = send(feats.at[rows_own : BLOCK + rows_own], feats.at[0:BLOCK], 1, after)
    to_before.start()
    to_after.start()
    edge_bufs = (edges_a, edges_b)
    term_bufs, first_bufs = (terms_a, terms_b), (first_a, first_b)
    sums_bufs = ((by_r_a, by_y_a), (by_r_b, by_y_b))

    def own_edges(b, buf):
        def put_edge(k, rows, cols_, value):
            buf[k, rows, cols_] = value
            if k == 0:
                rad_all[b, rows, cols_] = value

        def put_slope(rows, cols_, value):
            slope_all[b, rows, cols_] = value

        return edge_tasks(b + 1, 0, width, pos_i, pos_j, keep, put_edge, put_slope)

    msg[...] = jnp.zeros_like(msg)
    cols[...] = jnp.zeros_like(cols)
    dmsg[...] = jnp.zeros_like(dmsg)
    last = own_blocks - 1
    mingle(own_edges(0, edges_a), term_tasks(1, feats, weights, terms_a, first_a))

    def forward(i, carry):
        for half in range(2):
            b = i * 2 + half
            ahead = jnp.minimum(b + 1, last)
            mingle(
                message_tasks(b + 1, 0, width, edge_bufs[half], term_bufs[half], first_bufs[half], msg),
                own_edges(ahead, edge_bufs[1 - half]),
                term_tasks(ahead + 1, feats, weights, term_bufs[1 - half], first_bufs[1 - half]),
            )
        return carry

    lax.fori_loop(0, own_blocks // 2, forward, 0)

    to_before.wait()
    to_after.wait()
    halo = ((0, 2 * BLOCK), (own_blocks + 1, 0))
    for side, (e, low) in enumerate(halo):
        def put_edge(k, rows, cols_, value):
            edges_h[side, k, rows, cols_] = value

        def put_slope(rows, cols_, value):
            slopes_h[side, rows, cols_] = value

        mingle(
            edge_tasks(e, low, BLOCK, pos_i, pos_j, keep, put_edge, put_slope),
            term_tasks(e, feats, weights, term_bufs[side], first_bufs[side]),
        )
    for side, (e, low) in enumerate(halo):
        mingle(
            message_tasks(e, low, BLOCK, edges_h.at[side], term_bufs[side], first_bufs[side], msg)
        )

    size = 2 * BLOCK

    def atoms(i, carry):
        rows = pl.ds(pl.multiple_of(i * size + 2 * BLOCK, size), size)
        own = pl.ds(pl.multiple_of(i * size, size), size)
        ext = pl.ds(pl.multiple_of(i * size + BLOCK, BLOCK), size)
        slot = lax.broadcasted_iota(jnp.int32, (BLOCK, 1), 0)
        live = jnp.concatenate(
            [(slot < count[2 * i + step]).astype(F32) for step in range(2)], axis=0
        )
        m = [msg[k, rows, :] for k in range(9)]
        first = m[1] * m[1] + m[2] * m[2] + m[3] * m[3]
        second = m[4] * m[4] + m[5] * m[5] + m[6] * m[6] + m[7] * m[7] + m[8] * m[8]
        g0, g1, g2 = (gains[own, l * CH : (l + 1) * CH] for l in range(3))
        basis = m[0] + g0 * (m[0] * m[0]) + g1 * first + g2 * second
        mixed = mm(basis.astype(BF16), mix[...]) + mm(feats[ext, 0:CH], self_w[...])
        new_out[own, :] = (mixed * live).astype(BF16)
        gate = 1.0 / (1.0 + jnp.exp(-mixed))
        value = mixed * gate
        energy = live * jnp.sum(readout[...] * value, axis=1, keepdims=True)
        slope = live * readout[...] * (gate + value * (1.0 - gate))
        dbasis = mm_t(slope.astype(BF16), mix[...]).astype(BF16).astype(F32)
        dmsg[rows, 0:CH] = (dbasis * (1.0 + 2.0 * g0 * m[0])).astype(BF16)
        for k in range(1, 9):
            gain = g1 if k < 4 else g2
            dmsg[rows, k * CH : (k + 1) * CH] = (2.0 * dbasis * gain * m[k]).astype(BF16)
        lane = lax.broadcasted_iota(jnp.int32, (size, CH), 1)
        cols[rows, :] = jnp.where(lane == 3, energy, 0.0)
        return carry

    lax.fori_loop(0, own_blocks // 2, atoms, 0)

    for side, (e, low) in enumerate(halo):
        mingle(
            pull_tasks(
                e, low, BLOCK, edges_h.at[side, 0], slopes_h.at[side], term_bufs[side],
                first_bufs[side], dmsg, *sums_bufs[side],
            )
        )
    for side, (e, low) in enumerate(halo):
        mingle(force_tasks(e, low, BLOCK, *sums_bufs[side], pos_i, pos_j, keep, cols, nbr_out))
    force_before = send(nbr_out.at[0], inbox.at[0], 2, before)
    force_after = send(nbr_out.at[own_blocks + 1], inbox.at[1], 3, after)
    force_before.start()
    force_after.start()
    mingle(term_tasks(1, feats, weights, terms_a, first_a))

    def pull(b, half):
        return pull_tasks(
            b + 1, 0, width, rad_all.at[b], slope_all.at[b], term_bufs[half], first_bufs[half],
            dmsg, *sums_bufs[half],
        )

    def ahead_terms(b, half):
        return term_tasks(b + 1, feats, weights, term_bufs[half], first_bufs[half])

    def force(b, half):
        return force_tasks(
            b + 1, 0, width, *sums_bufs[half], pos_i, pos_j, keep, cols, nbr_out
        )

    mingle(pull(0, 0), ahead_terms(1, 1))

    def backward(i, carry):
        b = i * 2 + 1
        mingle(pull(b, 1), force(b - 1, 0), ahead_terms(b + 1, 0))
        mingle(pull(b + 1, 0), force(b, 1), ahead_terms(jnp.minimum(b + 2, last), 1))
        return carry

    lax.fori_loop(0, own_blocks // 2 - 1, backward, 0)
    mingle(pull(last, 1), force(last - 1, 0))
    mingle(force(last, 1))
    force_before.wait()
    force_after.wait()
    nbr_out[1] += inbox[1]
    nbr_out[own_blocks] += inbox[0]
    half_lane = lax.broadcasted_iota(jnp.int32, (8, CH), 1) < BLOCK
    for i in range(own_blocks // 2):
        lanes = slice(i * CH, (i + 1) * CH)
        flat = jnp.transpose(cols[2 * BLOCK + i * CH : 2 * BLOCK + (i + 1) * CH, :])[0:8, :]
        even, odd_ = nbr_out[2 * i + 1], nbr_out[2 * i + 2]
        even = even + pltpu.roll(even, BLOCK, 1)
        odd_ = odd_ + pltpu.roll(odd_, BLOCK, 1)
        total = flat - jnp.where(half_lane, even, odd_)
        force_out[:, lanes] = total[0:3, :]
        energy_out[:, lanes] = total[3:4, :]


def block_stage(
    keep, count, arrival, live, received, pos_i, pos_j, gains, weights, mix, self_w, readout
):
    ext_blocks = pos_j.shape[0]
    own_rows = (ext_blocks - 2) * BLOCK
    pad_rows = pos_i.shape[0]
    vmem = pl.BlockSpec(memory_space=pltpu.VMEM)
    smem = pl.BlockSpec(memory_space=pltpu.SMEM)
    width, depth = 3 * BLOCK, NB * BLOCK
    return pl.pallas_call(
        block_kernel,
        out_shape=(
            jax.ShapeDtypeStruct((3, own_rows), F32),
            jax.ShapeDtypeStruct((1, own_rows), F32),
            jax.ShapeDtypeStruct((own_rows, CH), BF16),
        ),
        in_specs=[smem, smem] + [vmem] * 10,
        out_specs=(vmem, vmem, vmem),
        scratch_shapes=[
            pltpu.VMEM((own_rows, received.shape[0]), BF16),
            pltpu.VMEM((PIECE * received.shape[0] // 8, 2 * CH), BF16),
            pltpu.VMEM((own_rows + 2 * BLOCK, 9 * CH), BF16),
            pltpu.VMEM((ext_blocks, 8, CH), F32),
            pltpu.VMEM((2, 8, CH), F32),
            pltpu.VMEM((9, width, depth), BF16),
            pltpu.VMEM((9, width, depth), BF16),
            pltpu.VMEM((ext_blocks - 2, width, depth), BF16),
            pltpu.VMEM((ext_blocks - 2, width, depth), BF16),
            pltpu.VMEM((depth, 10 * CH), BF16),
            pltpu.VMEM((depth, 10 * CH), BF16),
            pltpu.VMEM((depth, 9 * CH), BF16),
            pltpu.VMEM((depth, 9 * CH), BF16),
            pltpu.VMEM((2, 9, BLOCK, depth), BF16),
            pltpu.VMEM((2, BLOCK, depth), BF16),
            pltpu.VMEM((9, pad_rows, CH), F32),
            pltpu.VMEM((pad_rows, 9 * CH), BF16),
            pltpu.VMEM((9, width, CH), BF16),
            pltpu.VMEM((9, width, CH), BF16),
            pltpu.VMEM((9, width, CH), BF16),
            pltpu.VMEM((9, width, CH), BF16),
            pltpu.VMEM((pad_rows, CH), F32),
            pltpu.VMEM((NB, 7, CH), BF16),
            pltpu.SemaphoreType.DMA((4,)),
            pltpu.SemaphoreType.DMA((4,)),
        ],
        compiler_params=pltpu.CompilerParams(
            vmem_limit_bytes=50 * 1024 * 1024, collective_id=0, has_side_effects=True
        ),
        name="block_stage",
    )(keep, count, arrival, live, received, pos_i, pos_j, gains, weights, mix, self_w, readout)


def ring_pairs(axes):
    count = math.prod(lax.axis_size(axis) for axis in axes)
    forward = [(i, i + 1) for i in range(count - 1)]
    backward = [(target, source) for source, target in forward]
    return forward, backward


def per_device(
    features_domain,
    arrival,
    positions,
    species,
    block_count,
    pair_block,
    radial_weights,
    species_weights,
    mix_weight,
    self_weight,
    readout,
):
    axes = ("dom", "blk")
    devices = lax.axis_size(axes)
    atom_rows, feature_cols = features_domain.shape
    blocks = atom_rows // BLOCK
    forward, backward = ring_pairs(axes)

    parcels = pack_stage(features_domain).reshape(devices, 8, 7 * CH)
    received = lax.all_to_all(parcels, axes, split_axis=0, concat_axis=0, tiled=True)
    received = received.reshape(devices * 8, 7 * CH)

    coords = positions.T
    low = lax.ppermute(coords[:, atom_rows - BLOCK :], axes, forward)
    high = lax.ppermute(coords[:, :BLOCK], axes, backward)
    coords_ext = jnp.concatenate([low, coords, high], axis=1)
    pos_i = jnp.pad(coords_ext, ((0, 5), (BLOCK, BLOCK))).T
    by_block = coords_ext.reshape(3, blocks + 2, BLOCK).transpose(1, 0, 2)
    pos_j = jnp.pad(jnp.concatenate([by_block, by_block], axis=2), ((0, 0), (0, 5), (0, 0)))
    listed = jnp.pad((pair_block >= 0).astype(F32), ((2, 2), (0, 0)))
    keep = jnp.stack(
        [listed[0 : blocks + 2, 2], listed[1 : blocks + 3, 1], listed[2 : blocks + 4, 0]], axis=1
    ).reshape(-1)
    live = (jnp.arange(BLOCK, dtype=jnp.int32)[None, :] < block_count[:, None]).astype(F32)
    total = species_weights.shape[0]
    one_hot = (species[:, None] == jnp.arange(total, dtype=jnp.int32)[None, :]).astype(F32)
    gains = jnp.dot(one_hot, species_weights.reshape(total, -1), precision=lax.Precision.HIGHEST)

    forces, energies, new_rows = block_stage(
        keep,
        block_count,
        arrival[:, None],
        live.reshape(atom_rows, 1),
        received,
        pos_i,
        pos_j,
        gains,
        radial_weights,
        mix_weight,
        self_weight,
        readout[None, :],
    )
    return (energies.reshape(atom_rows), forces.T, new_rows)


def solution(mesh):
    placed = (
        P(("dom", "blk"), None),
        P(("dom", "blk")),
        P(("dom", "blk"), None),
        P(("dom", "blk")),
        P(("dom", "blk")),
        P(("dom", "blk"), None),
        P(),
        P(),
        P(),
        P(),
        P(),
    )
    return jax.shard_map(
        per_device,
        mesh=mesh,
        in_specs=placed,
        out_specs=(P(("dom", "blk")), P(("dom", "blk"), None), P(("dom", "blk"), None)),
        check_vma=False,
    )
```

```python
import functools
import math

import jax
import jax.numpy as jnp
import numpy as np
from jax import lax
from jax.experimental import pallas as pl
from jax.experimental.pallas import tpu as pltpu
from jax.sharding import PartitionSpec as P

BLOCK = 64
CH = 128
ROOT_THREE = math.sqrt(3.0)
DOT_PATH = (0, 5, 5, 5, 6, 6, 6, 6, 6)
CARRY_PATH = (-1, 3, 3, 3, 4, 4, 4, 4, 4)
LIFT_PATH = (-1, 1, 1, 1, 2, 2, 2, 2, 2)
CHUNK = 16
NB = 8
PIECE = 6
F32 = jnp.float32
BF16 = jnp.bfloat16


def mm(a, b):
    return jnp.dot(a, b, preferred_element_type=F32)


def mm_t(a, b):
    return lax.dot_general(a, b, (((1,), (1,)), ((), ())), preferred_element_type=F32)


def sin_pi(u):
    u2 = u * u
    acc = jnp.full_like(u, -(math.pi**11) / math.factorial(11))
    for power in (9, 7, 5, 3, 1):
        sign = 1.0 if power % 4 == 1 else -1.0
        acc = acc * u2 + sign * math.pi**power / math.factorial(power)
    return acc * u


def cos_pi(u):
    u2 = u * u
    acc = jnp.full_like(u, math.pi**12 / math.factorial(12))
    for power in (10, 8, 6, 4, 2, 0):
        sign = 1.0 if power % 4 == 0 else -1.0
        acc = acc * u2 + sign * math.pi**power / math.factorial(power)
    return acc


def harmonics(dx, dy, dz, x2, y2, z2):
    return (
        None,
        dx,
        dy,
        dz,
        ROOT_THREE * (dx * dy),
        ROOT_THREE * (dy * dz),
        z2 - 0.5 * (x2 + y2),
        ROOT_THREE * (dz * dx),
        (0.5 * ROOT_THREE) * (x2 - y2),
    )


def geometry(e, row0, pos_i, pos_j, keep):
    start = pl.multiple_of(e * BLOCK + row0, CHUNK)
    centre = pos_i[pl.ds(start, CHUNK), :]
    nbr = pos_j[e]
    dx = nbr[0:1, :] - centre[:, 0:1]
    dy = nbr[1:2, :] - centre[:, 1:2]
    dz = nbr[2:3, :] - centre[:, 2:3]
    x2, y2, z2 = dx * dx, dy * dy, dz * dz
    return dx, dy, dz, x2, y2, z2


def edge_tasks(e, low, width, pos_i, pos_j, keep, put_edge, put_slope):
    def task(row0):
        odd = lax.broadcasted_iota(jnp.int32, (CHUNK, CH), 1) >= BLOCK
        parity = odd.astype(F32)
        dx, dy, dz, x2, y2, z2 = geometry(e, row0, pos_i, pos_j, keep)
        s = x2 + y2 + z2
        t = jnp.maximum(1.0 - s, 0.0)
        t2 = t * t * keep[e * 3 + row0 // BLOCK]
        if row0 // BLOCK == 1:
            row = lax.broadcasted_iota(jnp.int32, (CHUNK, CH), 0) + row0 % BLOCK
            col = lax.broadcasted_iota(jnp.int32, (CHUNK, CH), 1) % BLOCK
            t2 = jnp.where(row == col, 0.0, t2)
        env = t2 * t
        denv = -3.0 * t2
        ys = harmonics(dx, dy, dz, x2, y2, z2)
        u = jnp.minimum(s, 1.0) - 0.5
        c1 = -sin_pi(u)
        s1 = cos_pi(u)
        c2 = 2.0 * c1 * c1 - 1.0
        s2 = 2.0 * c1 * s1
        two_c2 = 2.0 * c2
        c_before, c_now = jnp.where(odd, c1, c2), jnp.where(odd, c1, 1.0)
        s_before, s_now = jnp.where(odd, -s1, -s2), jnp.where(odd, s1, 0.0)
        rows = slice(row0 - low, row0 - low + CHUNK)
        ys = [None] + [y.astype(BF16) for y in ys[1:]]
        for m in range(4):
            cols = slice(m * CH, (m + 1) * CH)
            radial = (env * c_now).astype(BF16)
            order = math.pi * (2.0 * m + parity)
            put_slope(rows, cols, (denv * c_now - env * (order * s_now)).astype(BF16))
            put_edge(0, rows, cols, radial)
            for k in range(1, 9):
                put_edge(k, rows, cols, radial * ys[k])
            c_before, c_now = c_now, two_c2 * c_now - c_before
            s_before, s_now = s_now, two_c2 * s_now - s_before

    return [functools.partial(task, row0) for row0 in range(low, low + width, CHUNK)]


def mingle(main, *others):
    main = list(main)
    queue = [unit for other in others for unit in other]
    done = 0
    for position, step in enumerate(main):
        step()
        upto = len(queue) * (position + 1) // len(main)
        while done < upto:
            queue[done]()
            done += 1


def term_tasks(e, feats, weights, terms, terms0):
    def task(row0, k):
        start = pl.multiple_of(e * BLOCK + row0, CHUNK)
        hk = feats[pl.ds(start, CHUNK), k * CH : (k + 1) * CH]
        for n in range(NB):
            rows = slice(n * BLOCK + row0, n * BLOCK + row0 + CHUNK)
            if k == 0:
                terms0[rows, 0:CH] = hk * weights[n, 0:1, :]
                for q in range(2):
                    terms[rows, (8 + q) * CH : (9 + q) * CH] = hk * weights[n, 1 + q : 2 + q, :]
            else:
                dot_w = weights[n, DOT_PATH[k] : DOT_PATH[k] + 1, :]
                carry_w = weights[n, CARRY_PATH[k] : CARRY_PATH[k] + 1, :]
                terms[rows, (k - 1) * CH : k * CH] = hk * dot_w
                terms0[rows, k * CH : (k + 1) * CH] = hk * carry_w

    return [functools.partial(task, row0, k) for k in range(9) for row0 in range(0, BLOCK, CHUNK)]


def pair_terms(terms, k):
    q = LIFT_PATH[k] - 1
    return jnp.concatenate(
        [terms[:, (k - 1) * CH : k * CH], terms[:, (8 + q) * CH : (9 + q) * CH]], axis=1
    )


def message_tasks(e, low, width, edges, terms, terms0, msg, off=0):
    part = slice(off, off + width)
    rows = pl.ds(pl.multiple_of(e * BLOCK + low, BLOCK), width)

    def scalar():
        msg[0, rows, :] += mm(edges[0, part, :], terms0[:, 0:CH])

    def carried(k):
        both = mm(edges[0, part, :], terms0[:, k * CH : (k + 2) * CH])
        msg[k, rows, :] += both[:, 0:CH]
        msg[k + 1, rows, :] += both[:, CH:]

    def paired(k):
        both = mm(edges[k, part, :], pair_terms(terms, k))
        msg[0, rows, :] += both[:, 0:CH]
        msg[k, rows, :] += both[:, CH:]

    return (
        [scalar]
        + [functools.partial(carried, k) for k in range(1, 9, 2)]
        + [functools.partial(paired, k) for k in range(1, 9)]
    )


def pull_tasks(e, low, width, radial, slope, terms, terms0, dmsg, by_r, by_y, off=0):
    part_rows = slice(off, off + width)
    centre = pl.ds(pl.multiple_of(e * BLOCK + low, BLOCK), width)

    def first():
        grad = mm_t(dmsg[centre, :], terms0[...]).astype(BF16)
        total = None
        for m in range(4):
            sl = slice(m * CH, (m + 1) * CH)
            part = slope[part_rows, sl] * grad[:, sl]
            total = part if total is None else total + part
        by_r[0, part_rows, :] = total

    def order(k):
        lhs = jnp.concatenate([dmsg[centre, 0:CH], dmsg[centre, k * CH : (k + 1) * CH]], axis=1)
        grad = mm_t(lhs, pair_terms(terms, k)).astype(BF16)
        total_r = None
        total_y = None
        for m in range(4):
            sl = slice(m * CH, (m + 1) * CH)
            part_r = slope[part_rows, sl] * grad[:, sl]
            part_y = radial[part_rows, sl] * grad[:, sl]
            total_r = part_r if total_r is None else total_r + part_r
            total_y = part_y if total_y is None else total_y + part_y
        by_r[k, part_rows, :] = total_r
        by_y[k, part_rows, :] = total_y

    return [first] + [functools.partial(order, k) for k in range(1, 9)]


def force_tasks(e, low, width, by_r, by_y, pos_i, pos_j, keep, cols, nbr_out):
    state = {"tot": [jnp.zeros((CHUNK, CH), F32) for _ in range(3)]}
    lane = lax.broadcasted_iota(jnp.int32, (CHUNK, CH), 1)

    def task(row0):
        rows = slice(row0 - low, row0 - low + CHUNK)
        dx, dy, dz, x2, y2, z2 = geometry(e, row0, pos_i, pos_j, keep)
        ys = harmonics(dx, dy, dz, x2, y2, z2)
        radial_sum = by_r[0, rows, :].astype(F32)
        for k in range(1, 9):
            radial_sum += ys[k] * by_r[k, rows, :].astype(F32)
        radial_sum *= 2.0
        gy = [None] + [by_y[k, rows, :].astype(F32) for k in range(1, 9)]
        along = radial_sum - gy[6]
        parts = (
            dx * along + gy[1] + ROOT_THREE * (dy * gy[4] + dz * gy[7] + dx * gy[8]),
            dy * along + gy[2] + ROOT_THREE * (dx * gy[4] + dz * gy[5] - dy * gy[8]),
            dz * (radial_sum + 2.0 * gy[6]) + gy[3] + ROOT_THREE * (dy * gy[5] + dx * gy[7]),
        )
        state["tot"] = [a + b for a, b in zip(state["tot"], parts)]
        sums = [jnp.sum(p, axis=1, keepdims=True) for p in parts]
        add = jnp.where(
            lane == 0, sums[0], jnp.where(lane == 1, sums[1], jnp.where(lane == 2, sums[2], 0.0))
        )
        at = pl.ds(pl.multiple_of(e * BLOCK + row0, CHUNK), CHUNK)
        cols[at, :] += add

    def finish():
        sub = lax.broadcasted_iota(jnp.int32, (8, CH), 0)
        sums = [jnp.sum(p, axis=0, keepdims=True) for p in state["tot"]]
        nbr_out[e] = jnp.where(
            sub == 0, sums[0], jnp.where(sub == 1, sums[1], jnp.where(sub == 2, sums[2], 0.0))
        )

    return [functools.partial(task, row0) for row0 in range(low, low + width, CHUNK)] + [finish]


def fill_pick(pick, slot_of, alive, width):
    for tile in range(width // CH):
        lane_id = lax.broadcasted_iota(jnp.int32, (slot_of.shape[0], CH), 1) + tile * CH
        pick[:, tile * CH : (tile + 1) * CH] = jnp.where(slot_of == lane_id, alive, 0.0).astype(BF16)


def pack_kernel(rows_in, out):
    group, source = 256, 256 // 8 * PIECE
    row = lax.broadcasted_iota(jnp.int32, (group, source), 0)
    col = lax.broadcasted_iota(jnp.int32, (group, source), 1)
    parcel, within = row // 8, row % 8
    plain = ((within < PIECE) & (col == parcel * PIECE + within)).astype(F32).astype(BF16)
    last = lax.broadcasted_iota(jnp.int32, (group, CH), 0) % 8 == PIECE + 1
    for t in range(7):
        cols = slice(t * CH, (t + 1) * CH)
        if t < PIECE:
            extra = ((within >= PIECE) & (col == parcel * PIECE + t)).astype(F32).astype(BF16)
        for g in range(out.shape[0] // group):
            at = slice(g * source, (g + 1) * source)
            value = mm(plain, rows_in[at, cols])
            if t < PIECE:
                both = mm(extra, rows_in[at, 7 * CH : 9 * CH])
                value += jnp.where(last, both[:, CH:], both[:, 0:CH])
            out[g * group : (g + 1) * group, cols] = value.astype(BF16)


def pack_stage(rows_in):
    vmem = pl.BlockSpec(memory_space=pltpu.VMEM)
    return pl.pallas_call(
        pack_kernel,
        out_shape=jax.ShapeDtypeStruct((rows_in.shape[0] // PIECE * 8, 7 * CH), BF16),
        in_specs=[vmem],
        out_specs=vmem,
        compiler_params=pltpu.CompilerParams(vmem_limit_bytes=16 * 1024 * 1024),
        name="pack_stage",
    )(rows_in)


def block_kernel(
    keep,
    count,
    arrival,
    live_in,
    received,
    pos_i,
    pos_j,
    gains,
    weights_in,
    mix,
    self_w,
    readout,
    force_out,
    energy_out,
    new_out,
    pick,
    sorted_rows,
    feats,
    nbr_out,
    inbox,
    edges_a,
    edges_b,
    rad_all,
    slope_all,
    terms_a,
    terms_b,
    first_a,
    first_b,
    edges_h,
    slopes_h,
    msg,
    dmsg,
    by_r_a,
    by_r_b,
    by_y_a,
    by_y_b,
    cols,
    weights,
    send_sems,
    recv_sems,
):
    own_blocks = pos_j.shape[0] - 2
    width = 3 * BLOCK
    weights[...] = weights_in[...].astype(BF16)
    inner = lax.axis_size("blk")
    ranks = lax.axis_size("dom") * inner
    me = lax.axis_index("dom") * inner + lax.axis_index("blk")

    def place(rank):
        return (rank // inner, lax.rem(rank, inner))

    after = place(lax.rem(me + 1, ranks))
    before = place(lax.rem(me + ranks - 1, ranks))

    def send(source, target, lane, device):
        return pltpu.make_async_remote_copy(
            src_ref=source,
            dst_ref=target,
            send_sem=send_sems.at[lane],
            recv_sem=recv_sems.at[lane],
            device_id=device,
            device_id_type=pl.DeviceIdType.MESH,
        )

    barrier = pltpu.get_barrier_semaphore()
    for device in (before, after):
        pl.semaphore_signal(barrier, inc=1, device_id=device, device_id_type=pl.DeviceIdType.MESH)

    rows_own = own_blocks * BLOCK
    index = arrival[...]
    parcel = index // PIECE
    within = index - parcel * PIECE
    alive = live_in[...]
    own_feats = slice(BLOCK, BLOCK + rows_own)
    senders = received.shape[0] // 8
    slot_of = within * senders + parcel
    fill_pick(pick, slot_of, alive, PIECE * senders)
    sub_id = lax.broadcasted_iota(jnp.int32, (senders, received.shape[0]), 0)
    row_id = lax.broadcasted_iota(jnp.int32, (senders, received.shape[0]), 1)
    for extra in range(2):
        take = (row_id == sub_id * 8 + (PIECE + extra)).astype(F32).astype(BF16)
        for low in range(0, PIECE * CH, 2 * CH):
            both = mm(take, received[:, low : low + 2 * CH]).astype(BF16)
            for step in range(2):
                r = low // CH + step
                sorted_rows[r * senders : (r + 1) * senders, extra * CH : (extra + 1) * CH] = both[
                    :, step * CH : (step + 1) * CH
                ]
    feats[own_feats, 7 * CH : 9 * CH] = mm(pick[:, 0 : PIECE * senders], sorted_rows[...]).astype(BF16)
    slot_of = parcel * 8 + within
    fill_pick(pick, slot_of, alive, received.shape[0])
    for low in range(0, 7 * CH, 2 * CH):
        high = min(low + 2 * CH, 7 * CH)
        feats[own_feats, low:high] = mm(pick[...], received[:, low:high]).astype(BF16)

    pl.semaphore_wait(barrier, 2)
    to_before = send(feats.at[BLOCK : 2 * BLOCK], feats.at[BLOCK + rows_own : 2 * BLOCK + rows_own], 0, before)
    to_after = send(feats.at[rows_own : BLOCK + rows_own], feats.at[0:BLOCK], 1, after)
    to_before.start()
    to_after.start()
    edge_bufs = (edges_a, edges_b)
    term_bufs, first_bufs = (terms_a, terms_b), (first_a, first_b)
    sums_bufs = ((by_r_a, by_y_a), (by_r_b, by_y_b))

    def own_edges(b, buf):
        def put_edge(k, rows, cols_, value):
            buf[k, rows, cols_] = value
            if k == 0:
                rad_all[b, rows, cols_] = value

        def put_slope(rows, cols_, value):
            slope_all[b, rows, cols_] = value

        return edge_tasks(b + 1, 0, width, pos_i, pos_j, keep, put_edge, put_slope)

    msg[...] = jnp.zeros_like(msg)
    cols[...] = jnp.zeros_like(cols)
    dmsg[...] = jnp.zeros_like(dmsg)
    last = own_blocks - 1
    halo = ((0, 2 * BLOCK), (own_blocks + 1, 0))
    mingle(own_edges(0, edges_a), term_tasks(1, feats, weights, terms_a, first_a))

    def ahead_work(b, half):
        return own_edges(b, edge_bufs[half]) + term_tasks(
            b + 1, feats, weights, term_bufs[half], first_bufs[half]
        )

    def message(b, half, low=0, size=width):
        return message_tasks(
            b + 1, low, size, edge_bufs[half], term_bufs[half], first_bufs[half], msg, low
        )

    def halo_edges(side):
        def put_edge(k, rows, cols_, value):
            edges_h[side, k, rows, cols_] = value

        def put_slope(rows, cols_, value):
            slopes_h[side, rows, cols_] = value

        e, low = halo[side]
        return edge_tasks(e, low, BLOCK, pos_i, pos_j, keep, put_edge, put_slope)

    def halo_terms(side):
        return term_tasks(halo[side][0], feats, weights, term_bufs[side], first_bufs[side])

    def halo_message(side):
        e, low = halo[side]
        return message_tasks(
            e, low, BLOCK, edges_h.at[side], term_bufs[side], first_bufs[side], msg
        )

    mingle(message(0, 0, BLOCK, 2 * BLOCK), ahead_work(1, 1))

    def forward(i, carry):
        b = i * 2 + 1
        mingle(message(b, 1), ahead_work(b + 1, 0))
        mingle(message(b + 1, 0), ahead_work(b + 2, 1))
        return carry

    lax.fori_loop(0, own_blocks // 2 - 1, forward, 0)
    mingle(message(last, 1, 0, 2 * BLOCK), halo_edges(0), halo_edges(1))

    to_before.wait()
    to_after.wait()
    mingle(halo_terms(0))
    mingle(halo_message(0), halo_terms(1))
    mingle(halo_message(1))

    size = 2 * BLOCK

    def atoms(i, carry):
        rows = pl.ds(pl.multiple_of(i * size + 2 * BLOCK, size), size)
        own = pl.ds(pl.multiple_of(i * size, size), size)
        ext = pl.ds(pl.multiple_of(i * size + BLOCK, BLOCK), size)
        slot = lax.broadcasted_iota(jnp.int32, (BLOCK, 1), 0)
        live = jnp.concatenate(
            [(slot < count[2 * i + step]).astype(F32) for step in range(2)], axis=0
        )
        m = [msg[k, rows, :] for k in range(9)]
        first = m[1] * m[1] + m[2] * m[2] + m[3] * m[3]
        second = m[4] * m[4] + m[5] * m[5] + m[6] * m[6] + m[7] * m[7] + m[8] * m[8]
        g0, g1, g2 = (gains[own, l * CH : (l + 1) * CH] for l in range(3))
        basis = m[0] + g0 * (m[0] * m[0]) + g1 * first + g2 * second
        mixed = mm(basis.astype(BF16), mix[...]) + mm(feats[ext, 0:CH], self_w[...])
        new_out[own, :] = (mixed * live).astype(BF16)
        gate = 1.0 / (1.0 + jnp.exp(-mixed))
        value = mixed * gate
        energy = live * jnp.sum(readout[...] * value, axis=1, keepdims=True)
        slope = live * readout[...] * (gate + value * (1.0 - gate))
        dbasis = mm_t(slope.astype(BF16), mix[...]).astype(BF16).astype(F32)
        dmsg[rows, 0:CH] = (dbasis * (1.0 + 2.0 * g0 * m[0])).astype(BF16)
        for k in range(1, 9):
            gain = g1 if k < 4 else g2
            dmsg[rows, k * CH : (k + 1) * CH] = (2.0 * dbasis * gain * m[k]).astype(BF16)
        lane = lax.broadcasted_iota(jnp.int32, (size, CH), 1)
        cols[rows, :] = jnp.where(lane == 3, energy, 0.0)
        return carry

    lax.fori_loop(0, own_blocks // 2, atoms, 0)

    def halo_pull(side):
        e, low = halo[side]
        return pull_tasks(
            e, low, BLOCK, edges_h.at[side, 0], slopes_h.at[side], term_bufs[side],
            first_bufs[side], dmsg, *sums_bufs[side],
        )

    def halo_force(side):
        e, low = halo[side]
        return force_tasks(e, low, BLOCK, *sums_bufs[side], pos_i, pos_j, keep, cols, nbr_out)

    mingle(halo_pull(0))
    mingle(
        halo_pull(1), halo_force(0), term_tasks(1, feats, weights, terms_a, first_a)
    )
    mingle(halo_force(1))
    force_before = send(nbr_out.at[0], inbox.at[0], 2, before)
    force_after = send(nbr_out.at[own_blocks + 1], inbox.at[1], 3, after)
    force_before.start()
    force_after.start()

    def pull(b, half, low=0, size=width):
        return pull_tasks(
            b + 1, low, size, rad_all.at[b], slope_all.at[b], term_bufs[half], first_bufs[half],
            dmsg, *sums_bufs[half], low,
        )

    def ahead_terms(b, half):
        return term_tasks(b + 1, feats, weights, term_bufs[half], first_bufs[half])

    def force(b, half, size=width):
        return force_tasks(
            b + 1, 0, size, *sums_bufs[half], pos_i, pos_j, keep, cols, nbr_out
        )

    for sums in sums_bufs[0]:
        sums[:, 0:BLOCK, :] = jnp.zeros((9, BLOCK, CH), BF16)
    mingle(pull(0, 0, BLOCK, 2 * BLOCK), ahead_terms(1, 1))

    def backward(i, carry):
        b = i * 2 + 1
        mingle(pull(b, 1), force(b - 1, 0), ahead_terms(b + 1, 0))
        mingle(pull(b + 1, 0), force(b, 1), ahead_terms(jnp.minimum(b + 2, last), 1))
        return carry

    lax.fori_loop(0, own_blocks // 2 - 1, backward, 0)
    mingle(pull(last, 1, 0, 2 * BLOCK), force(last - 1, 0))
    mingle(force(last, 1, 2 * BLOCK))
    force_before.wait()
    force_after.wait()
    nbr_out[1] += inbox[1]
    nbr_out[own_blocks] += inbox[0]
    half_lane = lax.broadcasted_iota(jnp.int32, (8, CH), 1) < BLOCK
    for i in range(own_blocks // 2):
        lanes = slice(i * CH, (i + 1) * CH)
        flat = jnp.transpose(cols[2 * BLOCK + i * CH : 2 * BLOCK + (i + 1) * CH, :])[0:8, :]
        even, odd_ = nbr_out[2 * i + 1], nbr_out[2 * i + 2]
        even = even + pltpu.roll(even, BLOCK, 1)
        odd_ = odd_ + pltpu.roll(odd_, BLOCK, 1)
        total = flat - jnp.where(half_lane, even, odd_)
        force_out[:, lanes] = total[0:3, :]
        energy_out[:, lanes] = total[3:4, :]


def block_stage(
    keep, count, arrival, live, received, pos_i, pos_j, gains, weights, mix, self_w, readout
):
    ext_blocks = pos_j.shape[0]
    own_rows = (ext_blocks - 2) * BLOCK
    pad_rows = pos_i.shape[0]
    vmem = pl.BlockSpec(memory_space=pltpu.VMEM)
    smem = pl.BlockSpec(memory_space=pltpu.SMEM)
    width, depth = 3 * BLOCK, NB * BLOCK
    return pl.pallas_call(
        block_kernel,
        out_shape=(
            jax.ShapeDtypeStruct((3, own_rows), F32),
            jax.ShapeDtypeStruct((1, own_rows), F32),
            jax.ShapeDtypeStruct((own_rows, CH), BF16),
        ),
        in_specs=[smem, smem] + [vmem] * 10,
        out_specs=(vmem, vmem, vmem),
        scratch_shapes=[
            pltpu.VMEM((own_rows, received.shape[0]), BF16),
            pltpu.VMEM((PIECE * received.shape[0] // 8, 2 * CH), BF16),
            pltpu.VMEM((own_rows + 2 * BLOCK, 9 * CH), BF16),
            pltpu.VMEM((ext_blocks, 8, CH), F32),
            pltpu.VMEM((2, 8, CH), F32),
            pltpu.VMEM((9, width, depth), BF16),
            pltpu.VMEM((9, width, depth), BF16),
            pltpu.VMEM((ext_blocks - 2, width, depth), BF16),
            pltpu.VMEM((ext_blocks - 2, width, depth), BF16),
            pltpu.VMEM((depth, 10 * CH), BF16),
            pltpu.VMEM((depth, 10 * CH), BF16),
            pltpu.VMEM((depth, 9 * CH), BF16),
            pltpu.VMEM((depth, 9 * CH), BF16),
            pltpu.VMEM((2, 9, BLOCK, depth), BF16),
            pltpu.VMEM((2, BLOCK, depth), BF16),
            pltpu.VMEM((9, pad_rows, CH), F32),
            pltpu.VMEM((pad_rows, 9 * CH), BF16),
            pltpu.VMEM((9, width, CH), BF16),
            pltpu.VMEM((9, width, CH), BF16),
            pltpu.VMEM((9, width, CH), BF16),
            pltpu.VMEM((9, width, CH), BF16),
            pltpu.VMEM((pad_rows, CH), F32),
            pltpu.VMEM((NB, 7, CH), BF16),
            pltpu.SemaphoreType.DMA((4,)),
            pltpu.SemaphoreType.DMA((4,)),
        ],
        compiler_params=pltpu.CompilerParams(
            vmem_limit_bytes=50 * 1024 * 1024, collective_id=0, has_side_effects=True
        ),
        name="block_stage",
    )(keep, count, arrival, live, received, pos_i, pos_j, gains, weights, mix, self_w, readout)


def ring_pairs(axes):
    count = math.prod(lax.axis_size(axis) for axis in axes)
    forward = [(i, i + 1) for i in range(count - 1)]
    backward = [(target, source) for source, target in forward]
    return forward, backward


def per_device(
    features_domain,
    arrival,
    positions,
    species,
    block_count,
    pair_block,
    radial_weights,
    species_weights,
    mix_weight,
    self_weight,
    readout,
):
    axes = ("dom", "blk")
    devices = lax.axis_size(axes)
    atom_rows, feature_cols = features_domain.shape
    blocks = atom_rows // BLOCK
    forward, backward = ring_pairs(axes)

    parcels = pack_stage(features_domain).reshape(devices, 8, 7 * CH)
    received = lax.all_to_all(parcels, axes, split_axis=0, concat_axis=0, tiled=True)
    received = received.reshape(devices * 8, 7 * CH)

    coords = positions.T
    low = lax.ppermute(coords[:, atom_rows - BLOCK :], axes, forward)
    high = lax.ppermute(coords[:, :BLOCK], axes, backward)
    coords_ext = jnp.concatenate([low, coords, high], axis=1)
    pos_i = jnp.pad(coords_ext, ((0, 5), (BLOCK, BLOCK))).T
    by_block = coords_ext.reshape(3, blocks + 2, BLOCK).transpose(1, 0, 2)
    pos_j = jnp.pad(jnp.concatenate([by_block, by_block], axis=2), ((0, 0), (0, 5), (0, 0)))
    listed = jnp.pad((pair_block >= 0).astype(F32), ((2, 2), (0, 0)))
    keep = jnp.stack(
        [listed[0 : blocks + 2, 2], listed[1 : blocks + 3, 1], listed[2 : blocks + 4, 0]], axis=1
    ).reshape(-1)
    live = (jnp.arange(BLOCK, dtype=jnp.int32)[None, :] < block_count[:, None]).astype(F32)
    total = species_weights.shape[0]
    one_hot = (species[:, None] == jnp.arange(total, dtype=jnp.int32)[None, :]).astype(F32)
    gains = jnp.dot(one_hot, species_weights.reshape(total, -1), precision=lax.Precision.HIGHEST)

    forces, energies, new_rows = block_stage(
        keep,
        block_count,
        arrival[:, None],
        live.reshape(atom_rows, 1),
        received,
        pos_i,
        pos_j,
        gains,
        radial_weights,
        mix_weight,
        self_weight,
        readout[None, :],
    )
    return (energies.reshape(atom_rows), forces.T, new_rows)


def solution(mesh):
    placed = (
        P(("dom", "blk"), None),
        P(("dom", "blk")),
        P(("dom", "blk"), None),
        P(("dom", "blk")),
        P(("dom", "blk")),
        P(("dom", "blk"), None),
        P(),
        P(),
        P(),
        P(),
        P(),
    )
    return jax.shard_map(
        per_device,
        mesh=mesh,
        in_specs=placed,
        out_specs=(P(("dom", "blk")), P(("dom", "blk"), None), P(("dom", "blk"), None)),
        check_vma=False,
    )
```

```python
import functools
import math

import jax
import jax.numpy as jnp
import numpy as np
from jax import lax
from jax.experimental import pallas as pl
from jax.experimental.pallas import tpu as pltpu
from jax.sharding import PartitionSpec as P

BLOCK = 64
CH = 128
ROOT_THREE = math.sqrt(3.0)
DOT_PATH = (0, 5, 5, 5, 6, 6, 6, 6, 6)
CARRY_PATH = (-1, 3, 3, 3, 4, 4, 4, 4, 4)
LIFT_PATH = (-1, 1, 1, 1, 2, 2, 2, 2, 2)
CHUNK = 16
NB = 8
PIECE = 6
F32 = jnp.float32
BF16 = jnp.bfloat16


def mm(a, b):
    return jnp.dot(a, b, preferred_element_type=F32)


def mm_t(a, b):
    return lax.dot_general(a, b, (((1,), (1,)), ((), ())), preferred_element_type=F32)


def sin_pi(u):
    u2 = u * u
    acc = jnp.full_like(u, -(math.pi**11) / math.factorial(11))
    for power in (9, 7, 5, 3, 1):
        sign = 1.0 if power % 4 == 1 else -1.0
        acc = acc * u2 + sign * math.pi**power / math.factorial(power)
    return acc * u


def cos_pi(u):
    u2 = u * u
    acc = jnp.full_like(u, math.pi**12 / math.factorial(12))
    for power in (10, 8, 6, 4, 2, 0):
        sign = 1.0 if power % 4 == 0 else -1.0
        acc = acc * u2 + sign * math.pi**power / math.factorial(power)
    return acc


def harmonics(dx, dy, dz, x2, y2, z2):
    return (
        None,
        dx,
        dy,
        dz,
        ROOT_THREE * (dx * dy),
        ROOT_THREE * (dy * dz),
        z2 - 0.5 * (x2 + y2),
        ROOT_THREE * (dz * dx),
        (0.5 * ROOT_THREE) * (x2 - y2),
    )


def geometry(e, row0, pos_i, pos_j, keep):
    start = pl.multiple_of(e * BLOCK + row0, CHUNK)
    centre = pos_i[pl.ds(start, CHUNK), :]
    nbr = pos_j[e]
    dx = nbr[0:1, :] - centre[:, 0:1]
    dy = nbr[1:2, :] - centre[:, 1:2]
    dz = nbr[2:3, :] - centre[:, 2:3]
    x2, y2, z2 = dx * dx, dy * dy, dz * dz
    return dx, dy, dz, x2, y2, z2


def edge_tasks(e, low, width, pos_i, pos_j, keep, put_edge, put_slope):
    def task(row0):
        odd = lax.broadcasted_iota(jnp.int32, (CHUNK, CH), 1) >= BLOCK
        parity = odd.astype(F32)
        dx, dy, dz, x2, y2, z2 = geometry(e, row0, pos_i, pos_j, keep)
        s = x2 + y2 + z2
        t = jnp.maximum(1.0 - s, 0.0)
        t2 = t * t * keep[e * 3 + row0 // BLOCK]
        if row0 // BLOCK == 1:
            row = lax.broadcasted_iota(jnp.int32, (CHUNK, CH), 0) + row0 % BLOCK
            col = lax.broadcasted_iota(jnp.int32, (CHUNK, CH), 1) % BLOCK
            t2 = jnp.where(row == col, 0.0, t2)
        env = t2 * t
        denv = -3.0 * t2
        ys = harmonics(dx, dy, dz, x2, y2, z2)
        u = jnp.minimum(s, 1.0) - 0.5
        c1 = -sin_pi(u)
        s1 = cos_pi(u)
        c2 = 2.0 * c1 * c1 - 1.0
        s2 = 2.0 * c1 * s1
        two_c2 = 2.0 * c2
        c_before, c_now = jnp.where(odd, c1, c2), jnp.where(odd, c1, 1.0)
        s_before, s_now = jnp.where(odd, -s1, -s2), jnp.where(odd, s1, 0.0)
        rows = slice(row0 - low, row0 - low + CHUNK)
        ys = [None] + [y.astype(BF16) for y in ys[1:]]
        for m in range(4):
            cols = slice(m * CH, (m + 1) * CH)
            radial = (env * c_now).astype(BF16)
            order = math.pi * (2.0 * m + parity)
            put_slope(rows, cols, (denv * c_now - env * (order * s_now)).astype(BF16))
            put_edge(0, rows, cols, radial)
            for k in range(1, 9):
                put_edge(k, rows, cols, radial * ys[k])
            c_before, c_now = c_now, two_c2 * c_now - c_before
            s_before, s_now = s_now, two_c2 * s_now - s_before

    return [functools.partial(task, row0) for row0 in range(low, low + width, CHUNK)]


def mingle(main, *others):
    main = list(main)
    queue = [unit for other in others for unit in other]
    done = 0
    for position, step in enumerate(main):
        step()
        upto = len(queue) * (position + 1) // len(main)
        while done < upto:
            queue[done]()
            done += 1


def term_tasks(e, feats, weights, terms, terms0):
    def task(row0, k):
        start = pl.multiple_of(e * BLOCK + row0, CHUNK)
        hk = feats[pl.ds(start, CHUNK), k * CH : (k + 1) * CH]
        for n in range(NB):
            rows = slice(n * BLOCK + row0, n * BLOCK + row0 + CHUNK)
            if k == 0:
                terms0[rows, 0:CH] = hk * weights[n, 0:1, :]
                for q in range(2):
                    terms[rows, (8 + q) * CH : (9 + q) * CH] = hk * weights[n, 1 + q : 2 + q, :]
            else:
                dot_w = weights[n, DOT_PATH[k] : DOT_PATH[k] + 1, :]
                carry_w = weights[n, CARRY_PATH[k] : CARRY_PATH[k] + 1, :]
                terms[rows, (k - 1) * CH : k * CH] = hk * dot_w
                terms0[rows, k * CH : (k + 1) * CH] = hk * carry_w

    return [functools.partial(task, row0, k) for k in range(9) for row0 in range(0, BLOCK, CHUNK)]


def pair_terms(terms, k):
    q = LIFT_PATH[k] - 1
    return jnp.concatenate(
        [terms[:, (k - 1) * CH : k * CH], terms[:, (8 + q) * CH : (9 + q) * CH]], axis=1
    )


def message_tasks(e, low, width, edges, terms, terms0, msg, off=0):
    part = slice(off, off + width)
    rows = pl.ds(pl.multiple_of(e * BLOCK + low, BLOCK), width)

    def scalar():
        msg[0, rows, :] += mm(edges[0, part, :], terms0[:, 0:CH])

    def carried(k):
        both = mm(edges[0, part, :], terms0[:, k * CH : (k + 2) * CH])
        msg[k, rows, :] += both[:, 0:CH]
        msg[k + 1, rows, :] += both[:, CH:]

    def paired(k):
        both = mm(edges[k, part, :], pair_terms(terms, k))
        msg[0, rows, :] += both[:, 0:CH]
        msg[k, rows, :] += both[:, CH:]

    return (
        [scalar]
        + [functools.partial(carried, k) for k in range(1, 9, 2)]
        + [functools.partial(paired, k) for k in range(1, 9)]
    )


def pull_tasks(e, low, width, radial, slope, terms, terms0, dmsg, by_r, by_y, off=0):
    part_rows = slice(off, off + width)
    centre = pl.ds(pl.multiple_of(e * BLOCK + low, BLOCK), width)

    def first():
        grad = mm_t(dmsg[centre, :], terms0[...]).astype(BF16)
        total = None
        for m in range(4):
            sl = slice(m * CH, (m + 1) * CH)
            part = slope[part_rows, sl] * grad[:, sl]
            total = part if total is None else total + part
        by_r[0, part_rows, :] = total

    def order(k):
        lhs = jnp.concatenate([dmsg[centre, 0:CH], dmsg[centre, k * CH : (k + 1) * CH]], axis=1)
        grad = mm_t(lhs, pair_terms(terms, k)).astype(BF16)
        total_r = None
        total_y = None
        for m in range(4):
            sl = slice(m * CH, (m + 1) * CH)
            part_r = slope[part_rows, sl] * grad[:, sl]
            part_y = radial[part_rows, sl] * grad[:, sl]
            total_r = part_r if total_r is None else total_r + part_r
            total_y = part_y if total_y is None else total_y + part_y
        by_r[k, part_rows, :] = total_r
        by_y[k, part_rows, :] = total_y

    return [first] + [functools.partial(order, k) for k in range(1, 9)]


def force_tasks(e, low, width, by_r, by_y, pos_i, pos_j, keep, cols, nbr_out):
    state = {"tot": [jnp.zeros((CHUNK, CH), F32) for _ in range(3)]}
    lane = lax.broadcasted_iota(jnp.int32, (CHUNK, CH), 1)

    def task(row0):
        rows = slice(row0 - low, row0 - low + CHUNK)
        dx, dy, dz, x2, y2, z2 = geometry(e, row0, pos_i, pos_j, keep)
        ys = harmonics(dx, dy, dz, x2, y2, z2)
        radial_sum = by_r[0, rows, :].astype(F32)
        for k in range(1, 9):
            radial_sum += ys[k] * by_r[k, rows, :].astype(F32)
        radial_sum *= 2.0
        gy = [None] + [by_y[k, rows, :].astype(F32) for k in range(1, 9)]
        along = radial_sum - gy[6]
        parts = (
            dx * along + gy[1] + ROOT_THREE * (dy * gy[4] + dz * gy[7] + dx * gy[8]),
            dy * along + gy[2] + ROOT_THREE * (dx * gy[4] + dz * gy[5] - dy * gy[8]),
            dz * (radial_sum + 2.0 * gy[6]) + gy[3] + ROOT_THREE * (dy * gy[5] + dx * gy[7]),
        )
        state["tot"] = [a + b for a, b in zip(state["tot"], parts)]
        sums = [jnp.sum(p, axis=1, keepdims=True) for p in parts]
        add = jnp.where(
            lane == 0, sums[0], jnp.where(lane == 1, sums[1], jnp.where(lane == 2, sums[2], 0.0))
        )
        at = pl.ds(pl.multiple_of(e * BLOCK + row0, CHUNK), CHUNK)
        cols[at, :] += add

    def finish():
        sub = lax.broadcasted_iota(jnp.int32, (8, CH), 0)
        sums = [jnp.sum(p, axis=0, keepdims=True) for p in state["tot"]]
        nbr_out[e] = jnp.where(
            sub == 0, sums[0], jnp.where(sub == 1, sums[1], jnp.where(sub == 2, sums[2], 0.0))
        )

    return [functools.partial(task, row0) for row0 in range(low, low + width, CHUNK)] + [finish]


def fill_pick(pick, slot_of, alive, width):
    for tile in range(width // CH):
        lane_id = lax.broadcasted_iota(jnp.int32, (slot_of.shape[0], CH), 1) + tile * CH
        pick[:, tile * CH : (tile + 1) * CH] = jnp.where(slot_of == lane_id, alive, 0.0).astype(BF16)


def pack_kernel(rows_in, out):
    group, source = 256, 256 // 8 * PIECE
    row = lax.broadcasted_iota(jnp.int32, (group, source), 0)
    col = lax.broadcasted_iota(jnp.int32, (group, source), 1)
    parcel, within = row // 8, row % 8
    plain = ((within < PIECE) & (col == parcel * PIECE + within)).astype(F32).astype(BF16)
    last = lax.broadcasted_iota(jnp.int32, (group, CH), 0) % 8 == PIECE + 1
    for pair in range(0, 7, 2):
        tiles = range(pair, min(pair + 2, 7))
        extras = [
            ((within >= PIECE) & (col == parcel * PIECE + t)).astype(F32).astype(BF16)
            for t in tiles
            if t < PIECE
        ]
        for g in range(out.shape[0] // group):
            at = slice(g * source, (g + 1) * source)
            value = mm(plain, rows_in[at, pair * CH : (pair + len(tiles)) * CH])
            for step, extra in enumerate(extras):
                both = mm(extra, rows_in[at, 7 * CH : 9 * CH])
                cols = slice((pair + step) * CH, (pair + step + 1) * CH)
                part = value[:, step * CH : (step + 1) * CH]
                part += jnp.where(last, both[:, CH:], both[:, 0:CH])
                out[g * group : (g + 1) * group, cols] = part.astype(BF16)
            if not extras:
                out[g * group : (g + 1) * group, pair * CH : (pair + 1) * CH] = value.astype(BF16)


def pack_stage(rows_in):
    vmem = pl.BlockSpec(memory_space=pltpu.VMEM)
    return pl.pallas_call(
        pack_kernel,
        out_shape=jax.ShapeDtypeStruct((rows_in.shape[0] // PIECE * 8, 7 * CH), BF16),
        in_specs=[vmem],
        out_specs=vmem,
        compiler_params=pltpu.CompilerParams(vmem_limit_bytes=16 * 1024 * 1024),
        name="pack_stage",
    )(rows_in)


def block_kernel(
    keep,
    count,
    arrival,
    live_in,
    received,
    pos_i,
    pos_j,
    gains,
    weights_in,
    mix,
    self_w,
    readout,
    force_out,
    energy_out,
    new_out,
    pick,
    sorted_rows,
    feats,
    nbr_out,
    inbox,
    edges_a,
    edges_b,
    rad_all,
    slope_all,
    terms_a,
    terms_b,
    first_a,
    first_b,
    edges_h,
    slopes_h,
    msg,
    dmsg,
    by_r_a,
    by_r_b,
    by_y_a,
    by_y_b,
    cols,
    weights,
    send_sems,
    recv_sems,
):
    own_blocks = pos_j.shape[0] - 2
    width = 3 * BLOCK
    weights[...] = weights_in[...].astype(BF16)
    inner = lax.axis_size("blk")
    ranks = lax.axis_size("dom") * inner
    me = lax.axis_index("dom") * inner + lax.axis_index("blk")

    def place(rank):
        return (rank // inner, lax.rem(rank, inner))

    after = place(lax.rem(me + 1, ranks))
    before = place(lax.rem(me + ranks - 1, ranks))

    def send(source, target, lane, device):
        return pltpu.make_async_remote_copy(
            src_ref=source,
            dst_ref=target,
            send_sem=send_sems.at[lane],
            recv_sem=recv_sems.at[lane],
            device_id=device,
            device_id_type=pl.DeviceIdType.MESH,
        )

    barrier = pltpu.get_barrier_semaphore()
    for device in (before, after):
        pl.semaphore_signal(barrier, inc=1, device_id=device, device_id_type=pl.DeviceIdType.MESH)

    rows_own = own_blocks * BLOCK
    index = arrival[...]
    parcel = index // PIECE
    within = index - parcel * PIECE
    alive = live_in[...]
    own_feats = slice(BLOCK, BLOCK + rows_own)
    senders = received.shape[0] // 8
    slot_of = within * senders + parcel
    fill_pick(pick, slot_of, alive, PIECE * senders)
    sub_id = lax.broadcasted_iota(jnp.int32, (senders, received.shape[0]), 0)
    row_id = lax.broadcasted_iota(jnp.int32, (senders, received.shape[0]), 1)
    for extra in range(2):
        take = (row_id == sub_id * 8 + (PIECE + extra)).astype(F32).astype(BF16)
        for low in range(0, PIECE * CH, 2 * CH):
            both = mm(take, received[:, low : low + 2 * CH]).astype(BF16)
            for step in range(2):
                r = low // CH + step
                sorted_rows[r * senders : (r + 1) * senders, extra * CH : (extra + 1) * CH] = both[
                    :, step * CH : (step + 1) * CH
                ]
    feats[own_feats, 7 * CH : 9 * CH] = mm(pick[:, 0 : PIECE * senders], sorted_rows[...]).astype(BF16)
    slot_of = parcel * 8 + within
    fill_pick(pick, slot_of, alive, received.shape[0])
    for low in range(0, 7 * CH, 2 * CH):
        high = min(low + 2 * CH, 7 * CH)
        feats[own_feats, low:high] = mm(pick[...], received[:, low:high]).astype(BF16)

    pl.semaphore_wait(barrier, 2)
    to_before = send(feats.at[BLOCK : 2 * BLOCK], feats.at[BLOCK + rows_own : 2 * BLOCK + rows_own], 0, before)
    to_after = send(feats.at[rows_own : BLOCK + rows_own], feats.at[0:BLOCK], 1, after)
    to_before.start()
    to_after.start()
    edge_bufs = (edges_a, edges_b)
    term_bufs, first_bufs = (terms_a, terms_b), (first_a, first_b)
    sums_bufs = ((by_r_a, by_y_a), (by_r_b, by_y_b))

    def own_edges(b, buf):
        def put_edge(k, rows, cols_, value):
            buf[k, rows, cols_] = value
            if k == 0:
                rad_all[b, rows, cols_] = value

        def put_slope(rows, cols_, value):
            slope_all[b, rows, cols_] = value

        return edge_tasks(b + 1, 0, width, pos_i, pos_j, keep, put_edge, put_slope)

    msg[...] = jnp.zeros_like(msg)
    cols[...] = jnp.zeros_like(cols)
    dmsg[...] = jnp.zeros_like(dmsg)
    last = own_blocks - 1
    halo = ((0, 2 * BLOCK), (own_blocks + 1, 0))
    mingle(own_edges(0, edges_a), term_tasks(1, feats, weights, terms_a, first_a))

    def ahead_work(b, half):
        return own_edges(b, edge_bufs[half]) + term_tasks(
            b + 1, feats, weights, term_bufs[half], first_bufs[half]
        )

    def message(b, half, low=0, size=width):
        return message_tasks(
            b + 1, low, size, edge_bufs[half], term_bufs[half], first_bufs[half], msg, low
        )

    def halo_edges(side):
        def put_edge(k, rows, cols_, value):
            edges_h[side, k, rows, cols_] = value

        def put_slope(rows, cols_, value):
            slopes_h[side, rows, cols_] = value

        e, low = halo[side]
        return edge_tasks(e, low, BLOCK, pos_i, pos_j, keep, put_edge, put_slope)

    def halo_terms(side):
        return term_tasks(halo[side][0], feats, weights, term_bufs[side], first_bufs[side])

    def halo_message(side):
        e, low = halo[side]
        return message_tasks(
            e, low, BLOCK, edges_h.at[side], term_bufs[side], first_bufs[side], msg
        )

    mingle(message(0, 0, BLOCK, 2 * BLOCK), ahead_work(1, 1))

    def forward(i, carry):
        b = i * 2 + 1
        mingle(message(b, 1), ahead_work(b + 1, 0))
        mingle(message(b + 1, 0), ahead_work(b + 2, 1))
        return carry

    lax.fori_loop(0, own_blocks // 2 - 1, forward, 0)
    mingle(message(last, 1, 0, 2 * BLOCK), halo_edges(0), halo_edges(1))

    to_before.wait()
    to_after.wait()
    mingle(halo_terms(0))
    mingle(halo_message(0), halo_terms(1))
    mingle(halo_message(1))

    size = 2 * BLOCK

    def atoms(i, carry):
        rows = pl.ds(pl.multiple_of(i * size + 2 * BLOCK, size), size)
        own = pl.ds(pl.multiple_of(i * size, size), size)
        ext = pl.ds(pl.multiple_of(i * size + BLOCK, BLOCK), size)
        slot = lax.broadcasted_iota(jnp.int32, (BLOCK, 1), 0)
        live = jnp.concatenate(
            [(slot < count[2 * i + step]).astype(F32) for step in range(2)], axis=0
        )
        m = [msg[k, rows, :] for k in range(9)]
        first = m[1] * m[1] + m[2] * m[2] + m[3] * m[3]
        second = m[4] * m[4] + m[5] * m[5] + m[6] * m[6] + m[7] * m[7] + m[8] * m[8]
        g0, g1, g2 = (gains[own, l * CH : (l + 1) * CH] for l in range(3))
        basis = m[0] + g0 * (m[0] * m[0]) + g1 * first + g2 * second
        mixed = mm(basis.astype(BF16), mix[...]) + mm(feats[ext, 0:CH], self_w[...])
        new_out[own, :] = (mixed * live).astype(BF16)
        gate = 1.0 / (1.0 + jnp.exp(-mixed))
        value = mixed * gate
        energy = live * jnp.sum(readout[...] * value, axis=1, keepdims=True)
        slope = live * readout[...] * (gate + value * (1.0 - gate))
        dbasis = mm_t(slope.astype(BF16), mix[...]).astype(BF16).astype(F32)
        dmsg[rows, 0:CH] = (dbasis * (1.0 + 2.0 * g0 * m[0])).astype(BF16)
        for k in range(1, 9):
            gain = g1 if k < 4 else g2
            dmsg[rows, k * CH : (k + 1) * CH] = (2.0 * dbasis * gain * m[k]).astype(BF16)
        lane = lax.broadcasted_iota(jnp.int32, (size, CH), 1)
        cols[rows, :] = jnp.where(lane == 3, energy, 0.0)
        return carry

    lax.fori_loop(0, own_blocks // 2, atoms, 0)

    def halo_pull(side):
        e, low = halo[side]
        return pull_tasks(
            e, low, BLOCK, edges_h.at[side, 0], slopes_h.at[side], term_bufs[side],
            first_bufs[side], dmsg, *sums_bufs[side],
        )

    def halo_force(side):
        e, low = halo[side]
        return force_tasks(e, low, BLOCK, *sums_bufs[side], pos_i, pos_j, keep, cols, nbr_out)

    mingle(halo_pull(0))
    mingle(
        halo_pull(1), halo_force(0), term_tasks(1, feats, weights, terms_a, first_a)
    )
    mingle(halo_force(1))
    force_before = send(nbr_out.at[0], inbox.at[0], 2, before)
    force_after = send(nbr_out.at[own_blocks + 1], inbox.at[1], 3, after)
    force_before.start()
    force_after.start()

    def pull(b, half, low=0, size=width):
        return pull_tasks(
            b + 1, low, size, rad_all.at[b], slope_all.at[b], term_bufs[half], first_bufs[half],
            dmsg, *sums_bufs[half], low,
        )

    def ahead_terms(b, half):
        return term_tasks(b + 1, feats, weights, term_bufs[half], first_bufs[half])

    def force(b, half, size=width):
        return force_tasks(
            b + 1, 0, size, *sums_bufs[half], pos_i, pos_j, keep, cols, nbr_out
        )

    for sums in sums_bufs[0]:
        sums[:, 0:BLOCK, :] = jnp.zeros((9, BLOCK, CH), BF16)
    mingle(pull(0, 0, BLOCK, 2 * BLOCK), ahead_terms(1, 1))

    def backward(i, carry):
        b = i * 2 + 1
        mingle(pull(b, 1), force(b - 1, 0), ahead_terms(b + 1, 0))
        mingle(pull(b + 1, 0), force(b, 1), ahead_terms(jnp.minimum(b + 2, last), 1))
        return carry

    lax.fori_loop(0, own_blocks // 2 - 1, backward, 0)
    mingle(pull(last, 1, 0, 2 * BLOCK), force(last - 1, 0))
    mingle(force(last, 1, 2 * BLOCK))
    force_before.wait()
    force_after.wait()
    nbr_out[1] += inbox[1]
    nbr_out[own_blocks] += inbox[0]
    half_lane = lax.broadcasted_iota(jnp.int32, (8, CH), 1) < BLOCK
    for i in range(own_blocks // 2):
        lanes = slice(i * CH, (i + 1) * CH)
        flat = jnp.transpose(cols[2 * BLOCK + i * CH : 2 * BLOCK + (i + 1) * CH, :])[0:8, :]
        even, odd_ = nbr_out[2 * i + 1], nbr_out[2 * i + 2]
        even = even + pltpu.roll(even, BLOCK, 1)
        odd_ = odd_ + pltpu.roll(odd_, BLOCK, 1)
        total = flat - jnp.where(half_lane, even, odd_)
        force_out[:, lanes] = total[0:3, :]
        energy_out[:, lanes] = total[3:4, :]


def block_stage(
    keep, count, arrival, live, received, pos_i, pos_j, gains, weights, mix, self_w, readout
):
    ext_blocks = pos_j.shape[0]
    own_rows = (ext_blocks - 2) * BLOCK
    pad_rows = pos_i.shape[0]
    vmem = pl.BlockSpec(memory_space=pltpu.VMEM)
    smem = pl.BlockSpec(memory_space=pltpu.SMEM)
    width, depth = 3 * BLOCK, NB * BLOCK
    return pl.pallas_call(
        block_kernel,
        out_shape=(
            jax.ShapeDtypeStruct((3, own_rows), F32),
            jax.ShapeDtypeStruct((1, own_rows), F32),
            jax.ShapeDtypeStruct((own_rows, CH), BF16),
        ),
        in_specs=[smem, smem] + [vmem] * 10,
        out_specs=(vmem, vmem, vmem),
        scratch_shapes=[
            pltpu.VMEM((own_rows, received.shape[0]), BF16),
            pltpu.VMEM((PIECE * received.shape[0] // 8, 2 * CH), BF16),
            pltpu.VMEM((own_rows + 2 * BLOCK, 9 * CH), BF16),
            pltpu.VMEM((ext_blocks, 8, CH), F32),
            pltpu.VMEM((2, 8, CH), F32),
            pltpu.VMEM((9, width, depth), BF16),
            pltpu.VMEM((9, width, depth), BF16),
            pltpu.VMEM((ext_blocks - 2, width, depth), BF16),
            pltpu.VMEM((ext_blocks - 2, width, depth), BF16),
            pltpu.VMEM((depth, 10 * CH), BF16),
            pltpu.VMEM((depth, 10 * CH), BF16),
            pltpu.VMEM((depth, 9 * CH), BF16),
            pltpu.VMEM((depth, 9 * CH), BF16),
            pltpu.VMEM((2, 9, BLOCK, depth), BF16),
            pltpu.VMEM((2, BLOCK, depth), BF16),
            pltpu.VMEM((9, pad_rows, CH), F32),
            pltpu.VMEM((pad_rows, 9 * CH), BF16),
            pltpu.VMEM((9, width, CH), BF16),
            pltpu.VMEM((9, width, CH), BF16),
            pltpu.VMEM((9, width, CH), BF16),
            pltpu.VMEM((9, width, CH), BF16),
            pltpu.VMEM((pad_rows, CH), F32),
            pltpu.VMEM((NB, 7, CH), BF16),
            pltpu.SemaphoreType.DMA((4,)),
            pltpu.SemaphoreType.DMA((4,)),
        ],
        compiler_params=pltpu.CompilerParams(
            vmem_limit_bytes=50 * 1024 * 1024, collective_id=0, has_side_effects=True
        ),
        name="block_stage",
    )(keep, count, arrival, live, received, pos_i, pos_j, gains, weights, mix, self_w, readout)


def ring_pairs(axes):
    count = math.prod(lax.axis_size(axis) for axis in axes)
    forward = [(i, i + 1) for i in range(count - 1)]
    backward = [(target, source) for source, target in forward]
    return forward, backward


def per_device(
    features_domain,
    arrival,
    positions,
    species,
    block_count,
    pair_block,
    radial_weights,
    species_weights,
    mix_weight,
    self_weight,
    readout,
):
    axes = ("dom", "blk")
    devices = lax.axis_size(axes)
    atom_rows, feature_cols = features_domain.shape
    blocks = atom_rows // BLOCK
    forward, backward = ring_pairs(axes)

    parcels = pack_stage(features_domain).reshape(devices, 8, 7 * CH)
    received = lax.all_to_all(parcels, axes, split_axis=0, concat_axis=0, tiled=True)
    received = received.reshape(devices * 8, 7 * CH)

    coords = positions.T
    low = lax.ppermute(coords[:, atom_rows - BLOCK :], axes, forward)
    high = lax.ppermute(coords[:, :BLOCK], axes, backward)
    coords_ext = jnp.concatenate([low, coords, high], axis=1)
    pos_i = jnp.pad(coords_ext, ((0, 5), (BLOCK, BLOCK))).T
    by_block = coords_ext.reshape(3, blocks + 2, BLOCK).transpose(1, 0, 2)
    pos_j = jnp.pad(jnp.concatenate([by_block, by_block], axis=2), ((0, 0), (0, 5), (0, 0)))
    listed = jnp.pad((pair_block >= 0).astype(F32), ((2, 2), (0, 0)))
    keep = jnp.stack(
        [listed[0 : blocks + 2, 2], listed[1 : blocks + 3, 1], listed[2 : blocks + 4, 0]], axis=1
    ).reshape(-1)
    live = (jnp.arange(BLOCK, dtype=jnp.int32)[None, :] < block_count[:, None]).astype(F32)
    total = species_weights.shape[0]
    one_hot = (species[:, None] == jnp.arange(total, dtype=jnp.int32)[None, :]).astype(F32)
    gains = jnp.dot(one_hot, species_weights.reshape(total, -1), precision=lax.Precision.HIGHEST)

    forces, energies, new_rows = block_stage(
        keep,
        block_count,
        arrival[:, None],
        live.reshape(atom_rows, 1),
        received,
        pos_i,
        pos_j,
        gains,
        radial_weights,
        mix_weight,
        self_weight,
        readout[None, :],
    )
    return (energies.reshape(atom_rows), forces.T, new_rows)


def solution(mesh):
    placed = (
        P(("dom", "blk"), None),
        P(("dom", "blk")),
        P(("dom", "blk"), None),
        P(("dom", "blk")),
        P(("dom", "blk")),
        P(("dom", "blk"), None),
        P(),
        P(),
        P(),
        P(),
        P(),
    )
    return jax.shard_map(
        per_device,
        mesh=mesh,
        in_specs=placed,
        out_specs=(P(("dom", "blk")), P(("dom", "blk"), None), P(("dom", "blk"), None)),
        check_vma=False,
    )
```
